256 devices in a mesh: tm: 8 (over z_lo, core), chan: 32 (over z_hi, y, x).
Axes of the slice: x: 4, y: 4, z: 8 (z_hi: 2, z_lo: 4; z = z_hi * 4 + z_lo), core: 2. Of those that a mesh axis runs over, the one named last changes fastest.
Arguments:
- raw_strain: bfloat16 [256000, 4096], P('tm', 'chan'), may hold values from -600 to 600
- source_blocks: int32 [2], replicated, may hold values from 0 to 27, as said below
- band_bins: int32 [2], replicated, may hold values from 0 to 20, as said below
Outputs:
- cross_spectra: bfloat16 [1280, 2, 20, 4096], P('tm', None, None, 'chan')
The draws below stay inside these ranges and needn't reach their ends.
Inputs may be any that keep to these rules, and one draw needn't show every extreme that they name: `source_blocks`: each entry is the index of the channel block of 128 channels at which a virtual-source block of 640 channels begins; the two entries differ, one of them is always the last possible start, and the blocks may intersect. band_bins[0] is at most 2 and band_bins[1] is at least 18.
All inputs are finite; a program needn't handle non-finite values.
Results may differ from the reference program's by a relative error of at most 0.0091.
Values may be sent and summed in bfloat16 or wider, within the bound.
A program may use at most 64 MiB of HBM per device.

```python
import math
import jax
import jax.numpy as jnp
import numpy as np
from jax import lax

CH_DEV = 128
NW = 16
WIN = 500
NB = 20
VS = 640
TAPS = 64
DECIM = 4
CHANNELS = 4096
SAMPLES = 256000
WINDOWS = 128
SRC = 1280
SRC_STARTS = 28
N_TM = 8


def draw_raw_strain(key, part):
    streams = jax.random.split(key, 4)
    chan_scale = jnp.exp(jax.random.uniform(streams[0], (CHANNELS,), jnp.float32) * math.log(10.0))
    faded_mask = jax.random.randint(streams[1], (CHANNELS,), 0, 16) == 0
    chan_scale = jnp.where(faded_mask, 0.02, chan_scale)
    envelope = jnp.exp(jax.random.uniform(streams[2], (SAMPLES // WIN, CHANNELS), jnp.float32) * math.log(10.0))
    envelope = jnp.repeat(envelope, WIN, axis=0)
    background = jnp.clip(jax.random.normal(streams[3], (SAMPLES, CHANNELS), jnp.float32), -6.0, 6.0)
    return (background * chan_scale[None, :] * envelope).astype(jnp.bfloat16)


def draw_source_blocks(key, part):
    streams = jax.random.split(jax.random.fold_in(key, 17), 2)
    last_start = jnp.full((1,), SRC_STARTS - 1, jnp.int32)
    other_start = jax.random.randint(streams[0], (1,), 0, SRC_STARTS - 1)
    order_bit = jax.random.randint(streams[1], (1,), 0, 2)
    first_start = jnp.where(order_bit == 0, last_start, other_start)
    second_start = jnp.where(order_bit == 0, other_start, last_start)
    return jnp.concatenate([first_start, second_start]).astype(jnp.int32)


def draw_band_bins(key, part):
    streams = jax.random.split(key, 2)
    lower_edge = jax.random.randint(streams[0], (1,), 0, 3)
    upper_edge = jax.random.randint(streams[1], (1,), NB - 2, NB + 1)
    return jnp.concatenate([lower_edge, upper_edge]).astype(jnp.int32)


def setup_inputs(seed: int = 0) -> dict:
    key_list = jax.random.split(jax.random.key(seed), 4)
    raw_strain = draw_raw_strain(jax.random.fold_in(key_list[3], 71), 0)
    source_blocks = draw_source_blocks(jax.random.fold_in(key_list[3], 71), 0)
    band_bins = draw_band_bins(jax.random.fold_in(key_list[3], 71), 0)
    return {"raw_strain": raw_strain, "source_blocks": source_blocks, "band_bins": band_bins}


def lowpass_taps():
    offsets = np.arange(TAPS) - (TAPS - 1) / 2.0
    window = 0.54 - 0.46 * np.cos(2.0 * np.pi * np.arange(TAPS) / (TAPS - 1))
    angles = np.pi * 0.8 * offsets / DECIM
    values = np.sin(angles) / angles * window
    return values / values.sum()

def spectrum_table():
    time_ids = np.arange(WIN)
    freq_ids = np.arange(1, NB + 1)
    phases = 2.0 * np.pi * freq_ids[:, None] * time_ids[None, :] / WIN
    return jnp.asarray(np.concatenate([np.cos(phases), -np.sin(phases)], axis=0) / np.sqrt(WIN), jnp.bfloat16)

def reference(raw_strain, source_blocks, band_bins):
    tap_values = lax.optimization_barrier(jnp.asarray(lowpass_taps(), jnp.bfloat16)).astype(jnp.float32)
    decimated_len = SAMPLES // DECIM
    padded = jnp.concatenate([jnp.zeros((TAPS - DECIM, CHANNELS), jnp.float32), raw_strain.astype(jnp.float32)], axis=0)
    decimated = jnp.zeros((decimated_len, CHANNELS), jnp.float32)
    for tap_index in range(TAPS):
        start_row = TAPS - 1 - tap_index
        decimated = decimated + tap_values[tap_index] * lax.slice_in_dim(padded, start_row, start_row + DECIM * (decimated_len - 1) + 1, DECIM, 0)
    forget = math.exp(-1.0 / WIN)

    def advance(ema_state, energy_row):
        ema_state = forget * ema_state + (1.0 - forget) * energy_row
        return (ema_state, ema_state)
    final_state, running = lax.scan(advance, jnp.zeros((CHANNELS,), jnp.float32), decimated * decimated)
    normalized = (decimated / jnp.sqrt(jnp.maximum(running, 0.01))).astype(jnp.bfloat16)
    windows = normalized.reshape(WINDOWS, WIN, CHANNELS).astype(jnp.float32)
    dft_table = spectrum_table().astype(jnp.float32)
    spectra = jnp.einsum('kt,wtc->wkc', dft_table, windows)
    band_power = lax.optimization_barrier(jnp.sum(spectra * spectra, axis=1)) / NB
    bin_index = jnp.arange(NB)
    band_keep = ((bin_index >= band_bins[0]) & (bin_index < band_bins[1])).astype(jnp.float32)
    band_keep = jnp.concatenate([band_keep, band_keep])
    whitened = (spectra * band_keep[None, :, None] / jnp.sqrt(jnp.maximum(band_power, 0.1))[:, None, :]).astype(jnp.bfloat16)
    first_block = lax.dynamic_slice_in_dim(whitened, (source_blocks[0] * CH_DEV).astype(jnp.int32), VS, 2)
    second_block = lax.dynamic_slice_in_dim(whitened, (source_blocks[1] * CH_DEV).astype(jnp.int32), VS, 2)
    sources = jnp.concatenate([first_block, second_block], axis=2)
    own_spectra = whitened.reshape(N_TM, NW, 2, NB, CHANNELS).astype(jnp.float32)
    src_spectra = jnp.moveaxis(sources.reshape(N_TM, NW, 2, NB, SRC).astype(jnp.float32), 4, 0)
    stack_scale = 1.0 / math.sqrt(WINDOWS)

    def one_source(column):
        real_part = jnp.einsum('gwpkc,gwpk->gkc', own_spectra, column)
        imag_part = jnp.einsum('gwkc,gwk->gkc', own_spectra[:, :, 1], column[:, :, 0]) - jnp.einsum('gwkc,gwk->gkc', own_spectra[:, :, 0], column[:, :, 1])
        group_terms = jnp.stack([real_part, imag_part], axis=1) * stack_scale
        rounded = lax.optimization_barrier(group_terms.astype(jnp.bfloat16)).astype(jnp.float32)
        return lax.optimization_barrier(jnp.sum(rounded, axis=0)).astype(jnp.bfloat16)
    return lax.map(one_source, src_spectra)
```

```python
import functools
import math

import jax
import jax.numpy as jnp
import numpy as np
from jax import lax
from jax.experimental import pallas as pl
from jax.experimental.pallas import tpu as pltpu
from jax.sharding import PartitionSpec as P

NW = 16
WIN = 500
NB = 20
VS = 640
TAPS = 64
DECIM = 4
CH = 128
ROWS = DECIM * NW * WIN
OUTS = NW * WIN
MB = 112
KB = 512
STEP = DECIM * MB
PAIRS = 36
HALO = 64
RAW_PAD = HALO + 2 * PAIRS * STEP
DEC_PAD = 2 * PAIRS * MB
EB = 256
EN_PAD = 8192
CHUNKS = 5
CROWS = ROWS // CHUNKS
MAIN = 16
AR = 40
SR = 56
QR = 400
SHARE = 160
PARTS = ((0, 112), (112, 96), (208, 96), (304, 96))
FORGET = math.exp(-1.0 / WIN)
F32 = jnp.float32
BF16 = jnp.bfloat16
MESH = pl.DeviceIdType.MESH


def lowpass_taps():
    offsets = np.arange(TAPS) - (TAPS - 1) / 2.0
    window = 0.54 - 0.46 * np.cos(2.0 * np.pi * np.arange(TAPS) / (TAPS - 1))
    angles = np.pi * 0.8 * offsets / DECIM
    values = np.sin(angles) / angles * window
    return values / values.sum()


def tables():
    taps = lowpass_taps()
    lag = DECIM * np.arange(MB)[:, None] + DECIM - 1 + HALO - np.arange(KB)[None, :]
    decim = np.where((lag >= 0) & (lag < TAPS), taps[np.clip(lag, 0, TAPS - 1)], 0.0)
    gap = np.arange(EB)[:, None] - np.arange(EB)[None, :]
    within = np.where(gap >= 0, (1.0 - FORGET) * FORGET ** np.maximum(gap, 0), 0.0)
    rising = np.broadcast_to((FORGET ** (np.arange(EB) + 1.0))[:, None], (EB, CH))
    tail = OUTS - (2 * PAIRS - 1) * MB
    rows = np.arange(MB)
    full = (1.0 - FORGET) * FORGET ** (MB - 1.0 - rows)
    last = np.where(rows < tail, (1.0 - FORGET) * FORGET ** np.maximum(tail - 1.0 - rows, 0.0), 0.0)
    weights = np.broadcast_to(np.stack([full, last])[:, :, None], (2, MB, CH))
    phases = 2.0 * np.pi * np.arange(1, NB + 1)[:, None] * np.arange(WIN)[None, :] / WIN
    cos, sin = np.cos(phases) / np.sqrt(WIN), -np.sin(phases) / np.sqrt(WIN)
    ordered = np.concatenate([cos[:MAIN], sin[:MAIN], cos[MAIN:], sin[MAIN:]], axis=0)
    dft = np.zeros((4, 2 * NB, 512))
    for place in range(4):
        dft[place, :, 4 * place : 4 * place + WIN] = ordered
    return (
        jnp.asarray(decim, BF16),
        jnp.asarray(within, BF16),
        jnp.asarray(dft, BF16),
        jnp.asarray(rising, F32),
        jnp.asarray(weights, F32),
    )


def kernel(
    blocks_ref, band_ref, raw_ref, decim_ref, within_ref, dft_ref, rising_ref, weights_ref, out_ref,
    raw_v, dec_v, en_v, run_v, norm_v, white_v, total_v, totals_v, own_v, first_v, share_v, shares_v,
    pieces_v, acc_v,
    raw_sem, halo_sem, tot_ssem, tot_rsem, a_ssem, a_rsem, b_ssem, b_rsem, own_ssem, own_rsem,
    q_ssem, q_rsem,
):
    tm = lax.axis_index("tm")
    chan = lax.axis_index("chan")
    zl, core = tm // 2, tm % 2
    zh, pid = chan // 16, chan % 16
    y, x = pid // 4, pid % 4
    line = zh * 8 + tm

    def plane_peer(step):
        other = (pid + step) % 16
        return other, (tm, zh * 16 + other)

    def line_peer(step):
        other = (line + step) % 16
        return other, (other % 8, (other // 8) * 16 + pid)

    totals_v[...] = jnp.zeros(totals_v.shape, F32)

    barrier = pltpu.get_barrier_semaphore()
    for step in range(1, 16):
        pl.semaphore_signal(barrier, inc=1, device_id=plane_peer(step)[1], device_id_type=MESH)
        pl.semaphore_signal(barrier, inc=1, device_id=line_peer(step)[1], device_id_type=MESH)

    def chunk(c):
        return pltpu.make_async_copy(
            raw_ref.at[pl.ds(c * CROWS, CROWS)],
            raw_v.at[pl.ds(HALO + c * CROWS, CROWS)],
            raw_sem.at[c],
        )

    for c in range(CHUNKS):
        chunk(c).start()
    raw_v[HALO + ROWS : RAW_PAD, :] = jnp.zeros((RAW_PAD - HALO - ROWS, CH), BF16)
    en_v[DEC_PAD:EN_PAD, :] = jnp.zeros((EN_PAD - DEC_PAD, CH), BF16)
    dec_v[DEC_PAD:EN_PAD, :] = jnp.zeros((EN_PAD - DEC_PAD, CH), F32)

    @pl.when(tm == 0)
    def _():
        raw_v[0:HALO, :] = jnp.zeros((HALO, CH), BF16)

    def halo_to(other):
        return pltpu.make_async_remote_copy(
            src_ref=raw_ref.at[pl.ds(ROWS - HALO, HALO)],
            dst_ref=raw_v.at[pl.ds(0, HALO)],
            send_sem=halo_sem.at[0],
            recv_sem=halo_sem.at[1],
            device_id=(other, chan),
            device_id_type=MESH,
        )

    block_fade = FORGET**MB
    tail = OUTS - (2 * PAIRS - 1) * MB

    def decimate(pair, last):
        start = pl.multiple_of(pair * (2 * STEP), 128)
        left = raw_v[pl.ds(start, KB), :]
        right = raw_v[pl.ds(start + STEP, KB), :]
        both = jnp.dot(
            decim_ref[...], jnp.concatenate([left, right], axis=1), preferred_element_type=F32
        )
        row = pl.multiple_of(pair * (2 * MB), 32)
        sums = []
        for half in range(2):
            values = both[:, half * CH : (half + 1) * CH]
            dec_v[pl.ds(row + half * MB, MB), :] = values
            energy = values * values
            en_v[pl.ds(row + half * MB, MB), :] = energy.astype(BF16)
            weights = weights_ref[1 if (last and half == 1) else 0]
            sums.append(jnp.sum((weights * energy).reshape(MB // 8, 8, CH), axis=0))
        return sums[0] * (FORGET**tail if last else block_fade) + sums[1]

    def advance(pair, total):
        return total * (block_fade * block_fade) + decimate(pair, False)

    total = jnp.zeros((8, CH), F32)
    for c in range(CHUNKS):
        chunk(c).wait()
        if c == 2:
            pl.semaphore_wait(barrier, 30)

            @pl.when(tm < 7)
            def _():
                halo_to(tm + 1).start()

        total = lax.fori_loop(max(1, 7 * c), 7 * c + 7, advance, total)
    total = total * (block_fade * FORGET**tail) + decimate(PAIRS - 1, True)

    @pl.when(tm > 0)
    def _():
        halo_to(tm - 1).wait_recv()

    total = total + decimate(0, False) * FORGET ** (OUTS - 2 * MB)
    total_v[...] = jnp.broadcast_to(jnp.sum(total, axis=0, keepdims=True), (8, CH))

    def total_to(other, place, step):
        return pltpu.make_async_remote_copy(
            src_ref=total_v,
            dst_ref=totals_v.at[place],
            send_sem=tot_ssem.at[step],
            recv_sem=tot_rsem.at[place],
            device_id=(other, chan),
            device_id_type=MESH,
        )

    for step in range(1, 8):

        @pl.when(tm + step < 8)
        def _():
            total_to(tm + step, tm, step).start()

    def local_run(pair, carry):
        row = pl.multiple_of(pair * (2 * EB), 2 * EB)
        rhs = jnp.concatenate([en_v[pl.ds(row, EB), :], en_v[pl.ds(row + EB, EB), :]], axis=1)
        both = jnp.dot(within_ref[...], rhs, preferred_element_type=F32)
        run_v[pl.ds(row, EB), :] = both[:, :CH]
        run_v[pl.ds(row + EB, EB), :] = both[:, CH:]
        return carry

    lax.fori_loop(0, EN_PAD // (2 * EB), local_run, 0)

    for place in range(7):

        @pl.when(place < tm)
        def _():
            total_to(tm, place, 0).wait_recv()

    state = jnp.zeros((8, CH), F32)
    for place in range(7):
        state = jnp.where(place < tm, state * math.exp(-NW) + totals_v[place], state)

    def normalize(block, state):
        row = pl.multiple_of(block * EB, EB)
        running = run_v[pl.ds(row, EB), :] + rising_ref[...] * state[0:1, :]
        values = dec_v[pl.ds(row, EB), :] * lax.rsqrt(jnp.maximum(running, 0.01))
        norm_v[pl.ds(row, EB), :] = values.astype(BF16)
        return jnp.broadcast_to(running[EB - 1 : EB, :], (8, CH))

    lax.fori_loop(0, OUTS // EB + 1, normalize, state)

    low, high = band_ref[0], band_ref[1]
    row_id = lax.broadcasted_iota(jnp.int32, (2 * NB, CH), 0)
    bin_id = jnp.where(row_id < 2 * MAIN, row_id % MAIN, MAIN + row_id % 4)
    keep = jnp.where((bin_id >= low) & (bin_id < high), 1.0, 0.0).astype(F32)
    for first in range(NW):
        if first % 8 >= 4:
            continue
        start = (first * WIN) // 16 * 16
        rhs = jnp.concatenate(
            [norm_v[pl.ds(start, 512), :], norm_v[pl.ds(start + 4 * WIN, 512), :]], axis=1
        )
        both = jnp.dot(dft_ref[(first * WIN) % 16 // 4], rhs, preferred_element_type=F32)
        for half in range(2):
            w = first + 4 * half
            spectra = both[:, half * CH : (half + 1) * CH]
            power = jnp.sum(spectra * spectra, axis=0, keepdims=True) / NB
            white = spectra * keep * lax.rsqrt(jnp.maximum(power, 0.1))
            for p in range(2):
                white_v[pl.ds(p * NW + w, MAIN, stride=AR), :] = white[p * MAIN : (p + 1) * MAIN]
                white_v[pl.ds(w // 4 * (4 * AR) + 32 + p * 4 + w % 4, 4, stride=AR), :] = white[
                    32 + 4 * p : 36 + 4 * p
                ]
    own_v[tm] = white_v[...].reshape(MAIN, AR, CH).astype(BF16)

    def plane_copy(other, device, step, place):
        return pltpu.make_async_remote_copy(
            src_ref=own_v.at[tm, other],
            dst_ref=first_v.at[place],
            send_sem=a_ssem.at[step],
            recv_sem=a_rsem.at[place],
            device_id=device,
            device_id_type=MESH,
        )

    for step in range(1, 16):
        other, device = plane_peer(step)
        plane_copy(other, device, step, pid).start()

    def own_copy(group, other, slot):
        return pltpu.make_async_remote_copy(
            src_ref=own_v.at[group],
            dst_ref=own_v.at[group],
            send_sem=own_ssem.at[slot],
            recv_sem=own_rsem.at[group],
            device_id=(other, chan),
            device_id_type=MESH,
        )

    partner = zl * 2 + 1 - core
    sends = [(None, tm, partner, 0), (zl < 3, tm, tm + 2, 1), (zl > 0, tm, tm - 2, 2)]

    def start_send(entry):
        condition, group, other, slot = entry
        if condition is None:
            own_copy(group, other, slot).start()
        else:

            @pl.when(condition)
            def _():
                own_copy(group, other, slot).start()

    for entry in sends:
        start_send(entry)

    first_v[pid] = own_v[tm, pid]
    for step in range(1, 16):
        other, device = plane_peer(step)
        plane_copy(pid, device, 0, other).wait_recv()

    lane8 = lax.broadcasted_iota(jnp.int32, (8, CH), 1)
    lane40 = lax.broadcasted_iota(jnp.int32, (AR, CH), 1)
    for b in range(2):
        picked = []
        for i in range(5):
            block = blocks_ref[b] + i
            here = jnp.where(block // 16 == zh, 1.0, 0.0).astype(F32)
            picked.append(first_v[block % 16].astype(F32) * here)
        for jj in range(4):
            a, c = picked[jj], picked[jj + 1]
            if jj == 0:
                head = a
            else:
                turn = CH - 32 * jj
                head = jnp.where(
                    lane40 < turn, pltpu.roll(a, turn, axis=1), pltpu.roll(c, turn, axis=1)
                )
            rest = jnp.zeros((8, CH), F32)
            for q in range(5):
                turn = (32 * (q % 4) - 32 * jj) % CH
                part = c[8 * q : 8 * q + 8]
                part = pltpu.roll(part, turn, axis=1) if turn else part
                low_lane = 32 * (q % 4)
                part = jnp.where((lane8 >= low_lane) & (lane8 < low_lane + 32), part, 0.0)
                if q < 4:
                    rest = rest + part
                else:
                    last_rest = part
            share_v[b * 4 + jj] = jnp.concatenate([head, rest, last_rest], axis=0).astype(BF16)

    def line_copy(share, device, step, place):
        return pltpu.make_async_remote_copy(
            src_ref=share_v.at[share],
            dst_ref=shares_v.at[place],
            send_sem=b_ssem.at[step],
            recv_sem=b_rsem.at[place],
            device_id=device,
            device_id_type=MESH,
        )

    for step in range(1, 16):
        other, device = line_peer(step)
        line_copy(other % 8, device, step, line).start()
    shares_v[line] = share_v[tm]
    for step in range(1, 16):
        other, device = line_peer(step)
        line_copy(tm, device, 0, other).wait_recv()

    mains, tails = [], []
    for g in range(8):
        both = shares_v[g].astype(F32) + shares_v[8 + g].astype(F32)
        rests = []
        for q in range(5):
            packed = both[40:48] if q < 4 else both[48:56]
            turn = (CH - 32 * (q % 4)) % CH
            rests.append(pltpu.roll(packed, turn, axis=1) if turn else packed)
        rows = jnp.concatenate([both[0:40], jnp.concatenate(rests, axis=0)], axis=1)
        mains.append(rows[0:32])
        tails.append(rows[32:40])
    mains = jnp.concatenate(mains, axis=0).astype(BF16)
    tails = jnp.concatenate(tails + tails, axis=0).astype(BF16)
    eye = (
        lax.broadcasted_iota(jnp.int32, (SHARE, 256), 0)
        == lax.broadcasted_iota(jnp.int32, (SHARE, 256), 1)
    )
    eye = jnp.where(eye, 1.0, 0.0).astype(BF16)
    contract = (((1,), (1,)), ((), ()))
    turned = lax.dot_general(eye, mains, contract, preferred_element_type=F32)
    turned_tail = lax.dot_general(eye, tails, contract, preferred_element_type=F32)
    half_lane = lax.broadcasted_iota(jnp.int32, (80, CH), 1) < 64
    packed_tail = jnp.where(half_lane, turned_tail[0:80], turned_tail[80:160])
    pieces_v[pid] = jnp.concatenate([turned[:, :CH], turned[:, CH:], packed_tail], axis=0).astype(
        BF16
    )

    def at(dx, dy):
        return ((y + dy) % 4) * 4 + (x + dx) % 4

    def piece_copy(source, part, direction):
        dx, dy = ((1, 0), (3, 0), (0, 1), (0, 3))[direction]
        first, count = PARTS[part]
        rows = pl.ds(first, count)
        return pltpu.make_async_remote_copy(
            src_ref=pieces_v.at[source, rows],
            dst_ref=pieces_v.at[source, rows],
            send_sem=q_ssem.at[source, part, direction],
            recv_sem=q_rsem.at[source, part],
            device_id=(tm, zh * 16 + at(dx, dy)),
            device_id_type=MESH,
        )

    piece_sends = []

    def piece_send(source, part, direction):
        piece_copy(source, part, direction).start()
        piece_sends.append((source, part, direction))

    def piece_wait(source, part):
        piece_copy(source, part, 0).wait_recv()

    for part in range(4):
        axis = 0 if part < 2 else 2
        piece_send(pid, part, axis)
        piece_send(pid, part, axis + 1)
    for part in range(4):
        axis = 2 if part < 2 else 0
        piece_send(pid, part, axis)
        piece_send(pid, part, axis + 1)

    for step in range(1, 4):
        below, above = tm - 2 * step, tm + 2 * step

        @pl.when(zl - step >= 0)
        def _():
            own_copy(below, partner, 0).wait_recv()

        entry = (zl - step >= 0, below, partner, 3 * step)
        start_send(entry)
        sends.append(entry)
        if step < 3:
            entry = ((zl - step >= 0) & (zl < 3), below, tm + 2, 3 * step + 1)
            start_send(entry)
            sends.append(entry)

        @pl.when(zl + step <= 3)
        def _():
            own_copy(above, partner, 0).wait_recv()

        entry = (zl + step <= 3, above, partner, 9 + 3 * step)
        start_send(entry)
        sends.append(entry)
        if step < 3:
            entry = ((zl + step <= 3) & (zl > 0), above, tm - 2, 9 + 3 * step + 1)
            start_send(entry)
            sends.append(entry)
        if step == 1:
            relay_pieces(at, piece_send, piece_wait)
    finish_pieces(at, piece_send, piece_wait)

    for other_zl in range(4):
        own_copy(other_zl * 2 + 1 - core, partner, 0).wait_recv()

    scale = 1.0 / math.sqrt(8 * NW)

    def put(k, lhs, rhs):
        both = jnp.dot(lhs, rhs, preferred_element_type=F32) * scale
        acc_v[pl.ds(k, SHARE, stride=48), :] = both[:, :CH]
        acc_v[pl.ds(24 + k, SHARE, stride=48), :] = both[:, CH:]

    def main_bin(k, carry):
        lhs = jnp.concatenate([pieces_v[k, 0:SHARE], pieces_v[k, SHARE : 2 * SHARE]], axis=1)
        re, im = [], []
        for g in range(8):
            rows = own_v[g, k, 0:32]
            re.append(rows)
            im.append(rows[16:32])
            im.append(-rows[0:16])
        rhs = jnp.concatenate([jnp.concatenate(re, axis=0), jnp.concatenate(im, axis=0)], axis=1)
        put(k, lhs, rhs)
        return carry

    lax.fori_loop(0, MAIN, main_bin, 0)

    sign = jnp.where(lax.broadcasted_iota(jnp.int32, (8, CH), 0) < 4, 1.0, -1.0).astype(F32)

    def tail_bin(kk, carry):
        columns = []
        for pair in range(2):
            even = pieces_v[pair * 8 + kk, 2 * SHARE : QR].astype(F32)
            odd = pieces_v[pair * 8 + 4 + kk, 2 * SHARE : QR].astype(F32)
            upper = jnp.where(half_lane, even, pltpu.roll(odd, 64, axis=1))
            lower = jnp.where(half_lane, pltpu.roll(even, 64, axis=1), odd)
            columns.append(jnp.concatenate([upper, lower], axis=0))
        lhs = jnp.concatenate(columns, axis=1).astype(BF16)
        re, im = [], []
        for wh in range(4):
            for g in range(8):
                rows = own_v[g, wh * 4 + kk, 32:40].astype(F32)
                re.append(rows)
                im.append(pltpu.roll(rows, 4, axis=0) * sign)
        rhs = jnp.concatenate([jnp.concatenate(re, axis=0), jnp.concatenate(im, axis=0)], axis=1)
        put(MAIN + kk, lhs, rhs.astype(BF16))
        return carry

    lax.fori_loop(0, NB - MAIN, tail_bin, 0)

    def give(chunk_id, carry):
        row = pl.multiple_of(chunk_id * (8 * 48), 8 * 48)
        values = acc_v[pl.ds(row, 8 * 48), :].reshape(8, 2, 24, CH)
        out_ref[pl.ds(chunk_id * 8, 8)] = values[:, :, :NB, :].astype(BF16)
        return carry

    lax.fori_loop(0, SHARE // 8, give, 0)

    @pl.when(tm < 7)
    def _():
        halo_to(tm + 1).wait_send()

    for step in range(1, 8):

        @pl.when(tm + step < 8)
        def _():
            total_to(tm + step, tm, step).wait_send()

    for step in range(1, 16):
        other, device = plane_peer(step)
        plane_copy(other, device, step, pid).wait_send()
        other, device = line_peer(step)
        line_copy(other % 8, device, step, line).wait_send()
    for condition, group, other, slot in sends:
        if condition is None:
            own_copy(group, other, slot).wait_send()
        else:

            @pl.when(condition)
            def _():
                own_copy(group, other, slot).wait_send()

    for entry in piece_sends:
        piece_copy(*entry).wait_send()


def relay_pieces(at, send, wait):
    for part in range(4):
        along = 0 if part < 2 else 2
        across = 2 - along
        for toward in range(2):
            offset = 3 if toward == 0 else 1
            source = at(offset, 0) if along == 0 else at(0, offset)
            wait(source, part)
            if part % 2 == toward:
                send(source, part, along + toward)
            send(source, part, across)
            send(source, part, across + 1)


def finish_pieces(at, send, wait):
    for part in range(4):
        along = 0 if part < 2 else 2
        across = 2 - along

        def place(first, second):
            return at(first, second) if along == 0 else at(second, first)

        for first in (0, 1, 3, 2):
            if first == 2:
                source = place(2, 0)
                wait(source, part)
                send(source, part, across)
                send(source, part, across + 1)
            for toward in range(2):
                source = place(first, 3 if toward == 0 else 1)
                wait(source, part)
                if part % 2 == toward:
                    send(source, part, across + toward)
    for part in range(4):
        along = 0 if part < 2 else 2
        for first in range(4):
            wait(at(first, 2) if along == 0 else at(2, first), part)


def body(raw_strain, source_blocks, band_bins):
    decim, within, dft, rising, weights = tables()
    smem = pl.BlockSpec(memory_space=pltpu.SMEM)
    vmem = pl.BlockSpec(memory_space=pltpu.VMEM)
    dma = pltpu.SemaphoreType.DMA
    return pl.pallas_call(
        kernel,
        out_shape=jax.ShapeDtypeStruct((SHARE, 2, NB, CH), BF16),
        in_specs=[smem, smem, pl.BlockSpec(memory_space=pl.ANY), vmem, vmem, vmem, vmem, vmem],
        out_specs=vmem,
        scratch_shapes=[
            pltpu.VMEM((RAW_PAD, CH), BF16),
            pltpu.VMEM((EN_PAD, CH), F32),
            pltpu.VMEM((EN_PAD, CH), BF16),
            pltpu.VMEM((EN_PAD, CH), F32),
            pltpu.VMEM((EN_PAD, CH), BF16),
            pltpu.VMEM((MAIN * AR, CH), F32),
            pltpu.VMEM((8, CH), F32),
            pltpu.VMEM((8, 8, CH), F32),
            pltpu.VMEM((8, MAIN, AR, CH), BF16),
            pltpu.VMEM((16, AR, CH), BF16),
            pltpu.VMEM((8, SR, CH), BF16),
            pltpu.VMEM((16, SR, CH), BF16),
            pltpu.VMEM((16, QR, CH), BF16),
            pltpu.VMEM((SHARE * 48, CH), F32),
            dma((CHUNKS,)),
            dma((2,)),
            dma((8,)),
            dma((8,)),
            dma((16,)),
            dma((16,)),
            dma((16,)),
            dma((16,)),
            dma((20,)),
            dma((8,)),
            dma((16, 4, 4)),
            dma((16, 4)),
        ],
        compiler_params=pltpu.CompilerParams(
            collective_id=0, has_side_effects=True, vmem_limit_bytes=60 * 2**20
        ),
        name="cross_spectra",
    )(source_blocks, band_bins, raw_strain, decim, within, dft, rising, weights)


def solution(mesh):
    in_specs = (P("tm", "chan"), P(), P())
    out_specs = P("tm", None, None, "chan")
    return jax.shard_map(body, mesh=mesh, in_specs=in_specs, out_specs=out_specs, check_vma=False)
```

```python
import functools
import math

import jax
import jax.numpy as jnp
import numpy as np
from jax import lax
from jax.experimental import pallas as pl
from jax.experimental.pallas import tpu as pltpu
from jax.sharding import PartitionSpec as P

NW = 16
WIN = 500
NB = 20
VS = 640
TAPS = 64
DECIM = 4
CH = 128
ROWS = DECIM * NW * WIN
OUTS = NW * WIN
MB = 112
KB = 512
STEP = DECIM * MB
PAIRS = 36
HALO = 64
RAW_PAD = HALO + 2 * PAIRS * STEP
DEC_PAD = 2 * PAIRS * MB
EB = 256
EN_PAD = 8192
CHUNKS = (0, 7168, 13440, 19712, 25984, ROWS)
DR = 48
WITHIN = MB + 4 * DR
MAIN = 16
AR = 40
SR = 56
QR = 400
SHARE = 160
HR = QR // 2
FR = 104
FORGET = math.exp(-1.0 / WIN)
F32 = jnp.float32
BF16 = jnp.bfloat16
MESH = pl.DeviceIdType.MESH


def lowpass_taps():
    offsets = np.arange(TAPS) - (TAPS - 1) / 2.0
    window = 0.54 - 0.46 * np.cos(2.0 * np.pi * np.arange(TAPS) / (TAPS - 1))
    angles = np.pi * 0.8 * offsets / DECIM
    values = np.sin(angles) / angles * window
    return values / values.sum()


def table():
    taps = lowpass_taps()
    lag = DECIM * np.arange(MB)[:, None] + DECIM - 1 + HALO - np.arange(KB)[None, :]
    decim = np.where((lag >= 0) & (lag < TAPS), taps[np.clip(lag, 0, TAPS - 1)], 0.0)
    gap = np.arange(EB)[:, None] - np.arange(EB)[None, :]
    within = np.where(gap >= 0, (1.0 - FORGET) * FORGET ** np.maximum(gap, 0), 0.0)
    phases = 2.0 * np.pi * np.arange(1, NB + 1)[:, None] * np.arange(WIN)[None, :] / WIN
    cos, sin = np.cos(phases) / np.sqrt(WIN), -np.sin(phases) / np.sqrt(WIN)
    ordered = np.concatenate([cos[:MAIN], sin[:MAIN], cos[MAIN:], sin[MAIN:]], axis=0)
    dft = np.zeros((4, DR, 512))
    for place in range(4):
        dft[place, : 2 * NB, 4 * place : 4 * place + WIN] = ordered
    halves = np.concatenate([within[: EB // 2], within[EB // 2 :]], axis=1)
    return jnp.asarray(np.concatenate([decim, dft.reshape(4 * DR, 512), halves], axis=0), BF16)


def kernel(
    blocks_hbm, band_hbm, raw_ref, table_hbm, out_ref,
    blocks_ref, band_ref, table_v, raw_v, dec_v, en_v, run_v, norm_v, white_v, total_v, totals_v,
    own_v, first_v, share_v, shares_v, rows_v, pieces_v, rising_v, weights_v,
    small_sem, raw_sem, halo_sem, tot_sem, a_sem, b_sem, own_ssem, own_rsem, hand_sem, q_ssem, q_rsem,
):
    tm = lax.axis_index("tm")
    chan = lax.axis_index("chan")
    zl, core = tm // 2, tm % 2
    zh, pid = chan // 16, chan % 16
    y, x = pid // 4, pid % 4
    line = zh * 8 + tm
    totals_v[...] = jnp.zeros(totals_v.shape, F32)

    def repeat(count, step):
        lax.fori_loop(0, count, lambda n, carry: (step(n), carry)[1], 0)

    def plane_device(other):
        return (tm, zh * 16 + other)

    def line_device(other):
        return (other % 8, (other // 8) * 16 + pid)

    barrier = pltpu.get_barrier_semaphore()

    def greet(n):
        pl.semaphore_signal(
            barrier, inc=1, device_id=line_device((line + n + 1) % 16), device_id_type=MESH
        )
        pl.semaphore_signal(
            barrier, inc=1, device_id=plane_device((pid + n + 1) % 16), device_id_type=MESH
        )

    repeat(15, greet)

    def chunk(c):
        first, last = CHUNKS[c], CHUNKS[c + 1]
        return pltpu.make_async_copy(
            raw_ref.at[pl.ds(first, last - first)],
            raw_v.at[pl.ds(HALO + first, last - first)],
            raw_sem.at[c],
        )

    small = [
        pltpu.make_async_copy(source, target, small_sem.at[n])
        for n, (source, target) in enumerate(
            ((table_hbm, table_v), (blocks_hbm, blocks_ref), (band_hbm, band_ref))
        )
    ]
    small[0].start()
    for c in range(5):
        chunk(c).start()
    small[1].start()
    small[2].start()
    raw_v[HALO + ROWS : RAW_PAD, :] = jnp.zeros((RAW_PAD - HALO - ROWS, CH), BF16)
    en_v[DEC_PAD:EN_PAD, :] = jnp.zeros((EN_PAD - DEC_PAD, CH), BF16)
    dec_v[DEC_PAD:EN_PAD, :] = jnp.zeros((EN_PAD - DEC_PAD, CH), F32)

    @pl.when(tm == 0)
    def _():
        raw_v[0:HALO, :] = jnp.zeros((HALO, CH), BF16)

    def halo_to(other):
        return pltpu.make_async_remote_copy(
            src_ref=raw_ref.at[pl.ds(ROWS - HALO, HALO)],
            dst_ref=raw_v.at[pl.ds(0, HALO)],
            send_sem=halo_sem.at[0],
            recv_sem=halo_sem.at[1],
            device_id=(other, chan),
            device_id_type=MESH,
        )

    tail = OUTS - (2 * PAIRS - 1) * MB
    back = lax.broadcasted_iota(jnp.int32, (MB, CH), 0).astype(F32) - (MB - 1.0)
    weights_v[0] = (1.0 - FORGET) * jnp.exp(back * (1.0 / WIN))
    back = back + float(MB - tail)
    weights_v[1] = jnp.where(
        back <= 0.0, (1.0 - FORGET) * jnp.exp(jnp.minimum(back, 0.0) * (1.0 / WIN)), 0.0
    )
    place = lax.broadcasted_iota(jnp.int32, (EB, CH), 0).astype(F32)
    rising_v[...] = jnp.exp((place + 1.0) * (-1.0 / WIN))
    small[0].wait()

    block_fade = FORGET**MB
    tail_fade = FORGET**tail

    def decimate(n, total):
        pair = (n + 1) % PAIRS
        is_tail, is_first = pair == PAIRS - 1, pair == 0
        start = pl.multiple_of(pair * (2 * STEP), 128)
        left = raw_v[pl.ds(start, KB), :]
        right = raw_v[pl.ds(start + STEP, KB), :]
        both = jnp.dot(
            table_v[0:MB, :], jnp.concatenate([left, right], axis=1), preferred_element_type=F32
        )
        row = pl.multiple_of(pair * (2 * MB), 32)
        sums = []
        for half in range(2):
            values = both[:, half * CH : (half + 1) * CH]
            dec_v[pl.ds(row + half * MB, MB), :] = values
            energy = values * values
            en_v[pl.ds(row + half * MB, MB), :] = energy.astype(BF16)
            weights = weights_v[0] if half == 0 else weights_v[pair // (PAIRS - 1)]
            sums.append(jnp.sum((weights * energy).reshape(MB // 8, 8, CH), axis=0))
        fade = jnp.where(is_tail, tail_fade, block_fade).astype(F32)
        decay = jnp.where(is_first, 1.0, block_fade * fade).astype(F32)
        gain = jnp.where(is_first, FORGET ** (OUTS - 2 * MB), 1.0).astype(F32)
        return total * decay + (sums[0] * fade + sums[1]) * gain

    def stretch(c, total):
        for n in range(5):

            @pl.when(c == n)
            def _():
                chunk(n).wait()

        @pl.when(c == 4)
        def _():
            pl.semaphore_wait(barrier, 30)

            @pl.when(tm < 7)
            def _():
                halo_to(tm + 1).start()

        @pl.when((c == 5) & (tm > 0))
        def _():
            halo_to(tm - 1).wait_recv()

        return lax.fori_loop(7 * c, 7 * c + 7 - 6 * (c // 5), decimate, total)

    total = lax.fori_loop(0, 6, stretch, jnp.zeros((8, CH), F32))
    total_v[...] = jnp.broadcast_to(jnp.sum(total, axis=0, keepdims=True), (8, CH))

    def total_to(other):
        return pltpu.make_async_remote_copy(
            src_ref=total_v,
            dst_ref=totals_v.at[tm],
            send_sem=tot_sem.at[0],
            recv_sem=tot_sem.at[1],
            device_id=(other, chan),
            device_id_type=MESH,
        )

    repeat(7, lambda n: total_to((tm + n + 1) % 8).start())

    def arrived(ref, sem):
        pltpu.make_async_remote_copy(
            src_ref=ref, dst_ref=ref, send_sem=sem, recv_sem=sem,
            device_id=plane_device((pid + 1) % 16), device_id_type=MESH,
        ).wait_recv()

    def departed(ref, sem):
        pltpu.make_async_remote_copy(
            src_ref=ref, dst_ref=ref, send_sem=sem, recv_sem=sem,
            device_id=plane_device((pid + 1) % 16), device_id_type=MESH,
        ).wait_send()

    halves = table_v[WITHIN : WITHIN + EB // 2, :]
    within = jnp.concatenate([halves[:, :EB], halves[:, EB:]], axis=0)

    def local_run(n):
        row = pl.multiple_of(n * (2 * EB), 2 * EB)
        rhs = jnp.concatenate([en_v[pl.ds(row, EB), :], en_v[pl.ds(row + EB, EB), :]], axis=1)
        both = jnp.dot(within, rhs, preferred_element_type=F32)
        run_v[pl.ds(row, EB), :] = both[:, :CH]
        run_v[pl.ds(row + EB, EB), :] = both[:, CH:]

    repeat(EN_PAD // (2 * EB), local_run)
    arrived(totals_v.at[pl.ds(0, 7)], tot_sem.at[1])

    state = jnp.zeros((8, CH), F32)
    for group in range(7):
        state = jnp.where(group < tm, state * math.exp(-NW) + totals_v[group], state)

    def normalize(block, state):
        row = pl.multiple_of(block * EB, EB)
        running = run_v[pl.ds(row, EB), :] + rising_v[...] * state[0:1, :]
        values = dec_v[pl.ds(row, EB), :] * lax.rsqrt(jnp.maximum(running, 0.01))
        norm_v[pl.ds(row, EB), :] = values.astype(BF16)
        return jnp.broadcast_to(running[EB - 1 : EB, :], (8, CH))

    lax.fori_loop(0, OUTS // EB + 1, normalize, state)

    small[1].wait()
    small[2].wait()
    low, high = band_ref[0], band_ref[1]
    row_id = lax.broadcasted_iota(jnp.int32, (2 * NB, CH), 0)
    bin_id = jnp.where(row_id < 2 * MAIN, row_id % MAIN, MAIN + row_id % 4)
    keep = jnp.where((bin_id >= low) & (bin_id < high), 1.0, 0.0).astype(F32)

    def spectra_of(n):
        first = n + n // 4 * 4
        start = pl.multiple_of(first * WIN // 16 * 16, 16)
        rhs = jnp.concatenate(
            [norm_v[pl.ds(start, 512), :], norm_v[pl.ds(start + 4 * WIN, 512), :]], axis=1
        )
        part = pl.multiple_of(MB + first * WIN % 16 // 4 * DR, 16)
        both = jnp.dot(table_v[pl.ds(part, DR), :], rhs, preferred_element_type=F32)
        for half in range(2):
            w = first + 4 * half
            spectra = both[: 2 * NB, half * CH : (half + 1) * CH]
            power = jnp.sum(spectra * spectra, axis=0, keepdims=True) / NB
            white = spectra * keep * lax.rsqrt(jnp.maximum(power, 0.1))
            for p in range(2):
                white_v[pl.ds(p * NW + w, MAIN, stride=AR), :] = white[p * MAIN : (p + 1) * MAIN]
                white_v[pl.ds(w // 4 * (4 * AR) + 32 + p * 4 + w % 4, 4, stride=AR), :] = white[
                    32 + 4 * p : 36 + 4 * p
                ]

    repeat(8, spectra_of)
    own_v[tm] = white_v[...].reshape(MAIN, AR, CH).astype(BF16)

    def plane_copy(other):
        return pltpu.make_async_remote_copy(
            src_ref=own_v.at[tm, other],
            dst_ref=first_v.at[pid],
            send_sem=a_sem.at[0],
            recv_sem=a_sem.at[1],
            device_id=plane_device(other),
            device_id_type=MESH,
        )

    repeat(15, lambda n: plane_copy((pid + n + 1) % 16).start())

    def own_copy(group, other, slot, arrival):
        return pltpu.make_async_remote_copy(
            src_ref=own_v.at[group],
            dst_ref=own_v.at[group],
            send_sem=own_ssem.at[slot],
            recv_sem=arrival,
            device_id=(other, chan),
            device_id_type=MESH,
        )

    partner = zl * 2 + 1 - core

    def hand_over(group):
        return pltpu.make_async_remote_copy(
            src_ref=own_v.at[group],
            dst_ref=own_v.at[group],
            send_sem=hand_sem.at[0],
            recv_sem=hand_sem.at[1],
            device_id=(partner, chan),
            device_id_type=MESH,
        )

    sends = []

    def send_along(condition, group, other, slot):
        sends.append((condition, group, other, slot))

        @pl.when(condition)
        def _():
            own_copy(group, other, slot, own_rsem.at[group // 2]).start()

    send_along(zl < 3, tm, tm + 2, 0)
    send_along(zl > 0, tm, tm - 2, 1)
    hand_over(tm).start()

    def relay_own(step):
        below, above = tm - 2 * step, tm + 2 * step

        @pl.when(zl - step >= 0)
        def _():
            own_copy(below, partner, 0, own_rsem.at[below // 2]).wait_recv()

        @pl.when(zl + step <= 3)
        def _():
            own_copy(above, partner, 0, own_rsem.at[above // 2]).wait_recv()

        if step < 3:
            send_along((zl - step >= 0) & (zl < 3), below, tm + 2, 2 * step)
            send_along((zl + step <= 3) & (zl > 0), above, tm - 2, 2 * step + 1)

        @pl.when(zl - step >= 0)
        def _():
            hand_over(below).start()

        @pl.when(zl + step <= 3)
        def _():
            hand_over(above).start()

    first_v[pid] = own_v[tm, pid]
    arrived(first_v.at[pl.ds(0, 15)], a_sem.at[1])

    lane8 = lax.broadcasted_iota(jnp.int32, (8, CH), 1)
    lane40 = lax.broadcasted_iota(jnp.int32, (AR, CH), 1)

    def cut_share(share):
        jj = share % 4
        two = []
        for i in range(2):
            block = blocks_ref[share // 4] + jj + i
            here = jnp.where(block // 16 == zh, 1.0, 0.0).astype(F32)
            two.append(first_v[block % 16].astype(F32) * here)
        a, c = two
        turn = CH - 32 * jj
        head = jnp.where(
            lane40 < turn, pltpu.roll(a, turn % CH, axis=1), pltpu.roll(c, turn % CH, axis=1)
        )
        turned = pltpu.roll(c, (CH - 32 * jj) % CH, axis=1)
        rest = jnp.where(lane8 < 32, turned[0:8], 0.0)
        for q in range(1, 4):
            part = pltpu.roll(turned[8 * q : 8 * q + 8], 32 * q, axis=1)
            rest = jnp.where((lane8 >= 32 * q) & (lane8 < 32 * q + 32), part, rest)
        last_rest = jnp.where(lane8 < 32, turned[32:40], 0.0)
        share_v[share] = jnp.concatenate([head, rest, last_rest], axis=0).astype(BF16)

    repeat(8, cut_share)

    def line_copy(other):
        return pltpu.make_async_remote_copy(
            src_ref=share_v.at[other % 8],
            dst_ref=shares_v.at[line],
            send_sem=b_sem.at[0],
            recv_sem=b_sem.at[1],
            device_id=line_device(other),
            device_id_type=MESH,
        )

    repeat(15, lambda n: line_copy((line + n + 1) % 16).start())
    shares_v[line] = share_v[tm]
    relay_own(1)
    arrived(shares_v.at[pl.ds(0, 15)], b_sem.at[1])

    def unpack(g):
        both = shares_v[g].astype(F32) + shares_v[8 + g].astype(F32)
        rests = [both[40:48]]
        for q in range(1, 4):
            rests.append(pltpu.roll(both[40:48], CH - 32 * q, axis=1))
        rests.append(both[48:56])
        rows = jnp.concatenate([both[0:40], jnp.concatenate(rests, axis=0)], axis=1)
        rows_v[pl.ds(pl.multiple_of(g * 32, 32), 32), :] = rows[0:32]
        rows_v[pl.ds(pl.multiple_of(256 + g * 8, 8), 8), :] = rows[32:40]
        rows_v[pl.ds(pl.multiple_of(320 + g * 8, 8), 8), :] = rows[32:40]

    repeat(8, unpack)
    eye = (
        lax.broadcasted_iota(jnp.int32, (SHARE, 256), 0)
        == lax.broadcasted_iota(jnp.int32, (SHARE, 256), 1)
    )
    eye = jnp.where(eye, 1.0, 0.0).astype(BF16)
    turned = lax.dot_general(
        eye, rows_v[...].astype(BF16), (((1,), (1,)), ((), ())), preferred_element_type=F32
    )
    half_lane = lax.broadcasted_iota(jnp.int32, (80, CH), 1) < 64
    packed_tail = jnp.where(half_lane, turned[0:80, 2 * CH :], turned[80:160, 2 * CH :])
    pieces_v[pid] = jnp.concatenate(
        [turned[:, :CH], turned[:, CH : 2 * CH], packed_tail], axis=0
    ).astype(BF16)

    def at(h, f, s):
        dx, dy = f * (1 - h) + s * h, f * h + s * (1 - h)
        return ((y + dy) % 4) * 4 + (x + dx) % 4

    def piece_copy(h, f, s, along, across, first, count, event):
        rows = pl.ds(pl.multiple_of(h * HR + first, 8), count)
        return pltpu.make_async_remote_copy(
            src_ref=pieces_v.at[at(h, f, s), rows],
            dst_ref=pieces_v.at[at(h, f, s), rows],
            send_sem=q_ssem.at[0],
            recv_sem=q_rsem.at[event],
            device_id=plane_device(at(h, along, across)),
            device_id_type=MESH,
        )

    def wait_half(h, f, s, event):
        piece_copy(h, f, s, 1, 0, 0, HR, event).wait_recv()

    def send_across(h, f):
        for t in range(2):
            piece_copy(h, f, 0, 0, 1 + 2 * t, 0, HR, h * 11 + 3 + 2 * f + t).start()

    def forward(h, f, s, along, t, event):
        first, count = ((0, FR), (FR, HR - FR))[t]
        step = 1 + 2 * t
        piece_copy(
            h, f, s, step if along else 0, 0 if along else step, first, count, event
        ).start()

    def own_half(h):
        for t in range(2):
            piece_copy(h, 0, 0, 1 + 2 * t, 0, 0, HR, h * 11 + t).start()

    def near_along(h):
        for t in range(2):
            wait_half(h, 3 - 2 * t, 0, h * 11 + t)
            forward(h, 3 - 2 * t, 0, True, t, h * 11 + 2)
            send_across(h, 3 - 2 * t)

    def near_across(h, f):
        for t in range(2):
            wait_half(h, f, 3 - 2 * t, h * 11 + 3 + 2 * f + t)
            forward(h, f, 3 - 2 * t, False, t, 22)

    def far_along(h):
        wait_half(h, 2, 0, h * 11 + 2)
        send_across(h, 2)

    repeat(2, own_half)
    repeat(2, lambda h: send_across(h, 0))
    repeat(2, near_along)
    repeat(2, lambda h: near_across(h, 0))
    repeat(2, far_along)
    relay_own(2)
    repeat(6, lambda n: near_across(n % 2, n // 2 + 1))
    relay_own(3)
    arrived(own_v.at[pl.ds(0, 4)], hand_sem.at[1])

    scale = 1.0 / math.sqrt(8 * NW)

    def put(k, lhs, rhs):
        both = jnp.dot(lhs, rhs, preferred_element_type=F32) * scale
        out_ref[pl.ds(2 * k, SHARE, stride=2 * NB), :] = both[:, :CH]
        out_ref[pl.ds(2 * k + 1, SHARE, stride=2 * NB), :] = both[:, CH:]

    def main_bin(k):
        lhs = jnp.concatenate([pieces_v[k, 0:SHARE], pieces_v[k, SHARE : 2 * SHARE]], axis=1)
        re, im = [], []
        for g in range(8):
            rows = own_v[g, k, 0:32]
            re.append(rows)
            im.append(rows[16:32])
            im.append(-rows[0:16])
        rhs = jnp.concatenate([jnp.concatenate(re, axis=0), jnp.concatenate(im, axis=0)], axis=1)
        put(k, lhs, rhs)

    def near_bin(n):
        f, s = n % 3, n // 3
        main_bin(at(0, f + f // 2, s + s // 2))

    def far_bin(n):
        late, m = n // 4, n % 4
        main_bin(at(0, 2 * (1 - late) + late * (m + m // 2), m * (1 - late) + 2 * late))

    repeat(9, near_bin)
    arrived(pieces_v.at[pl.ds(0, 4)], q_rsem.at[22])
    repeat(7, far_bin)

    sign = jnp.where(lax.broadcasted_iota(jnp.int32, (8, CH), 0) < 4, 1.0, -1.0).astype(F32)

    def tail_bin(kk):
        columns = []
        for pair in range(2):
            even = pieces_v[pair * 8 + kk, 2 * SHARE : QR].astype(F32)
            odd = pieces_v[pair * 8 + 4 + kk, 2 * SHARE : QR].astype(F32)
            upper = jnp.where(half_lane, even, pltpu.roll(odd, 64, axis=1))
            lower = jnp.where(half_lane, pltpu.roll(even, 64, axis=1), odd)
            columns.append(jnp.concatenate([upper, lower], axis=0))
        lhs = jnp.concatenate(columns, axis=1).astype(BF16)
        re, im = [], []
        for wh in range(4):
            for g in range(8):
                rows = own_v[g, wh * 4 + kk, 32:40].astype(F32)
                re.append(rows)
                im.append(pltpu.roll(rows, 4, axis=0) * sign)
        rhs = jnp.concatenate([jnp.concatenate(re, axis=0), jnp.concatenate(im, axis=0)], axis=1)
        put(MAIN + kk, lhs, rhs.astype(BF16))

    repeat(NB - MAIN, tail_bin)

    @pl.when(tm < 7)
    def _():
        halo_to(tm + 1).wait_send()

    departed(totals_v.at[pl.ds(0, 7)], tot_sem.at[0])
    departed(first_v.at[pl.ds(0, 15)], a_sem.at[0])
    departed(shares_v.at[pl.ds(0, 15)], b_sem.at[0])
    departed(own_v.at[pl.ds(0, 4)], hand_sem.at[0])
    departed(pieces_v.at[pl.ds(0, 15)], q_ssem.at[0])
    for condition, group, other, slot in sends:

        @pl.when(condition)
        def _():
            own_copy(group, other, slot, own_rsem.at[0]).wait_send()


def body(raw_strain, source_blocks, band_bins):
    hbm = pl.BlockSpec(memory_space=pltpu.HBM)
    vmem = pl.BlockSpec(memory_space=pltpu.VMEM)
    dma = pltpu.SemaphoreType.DMA
    rows = pl.pallas_call(
        kernel,
        out_shape=jax.ShapeDtypeStruct((SHARE * NB * 2, CH), F32),
        in_specs=[hbm] * 4,
        out_specs=vmem,
        scratch_shapes=[
            pltpu.SMEM((2,), jnp.int32),
            pltpu.SMEM((2,), jnp.int32),
            pltpu.VMEM((WITHIN + EB // 2, 512), BF16),
            pltpu.VMEM((RAW_PAD, CH), BF16),
            pltpu.VMEM((EN_PAD, CH), F32),
            pltpu.VMEM((EN_PAD, CH), BF16),
            pltpu.VMEM((EN_PAD, CH), F32),
            pltpu.VMEM((EN_PAD, CH), BF16),
            pltpu.VMEM((MAIN * AR, CH), F32),
            pltpu.VMEM((8, CH), F32),
            pltpu.VMEM((8, 8, CH), F32),
            pltpu.VMEM((8, MAIN, AR, CH), BF16),
            pltpu.VMEM((16, AR, CH), BF16),
            pltpu.VMEM((8, SR, CH), BF16),
            pltpu.VMEM((16, SR, CH), BF16),
            pltpu.VMEM((384, 256), F32),
            pltpu.VMEM((16, QR, CH), BF16),
            pltpu.VMEM((EB, CH), F32),
            pltpu.VMEM((2, MB, CH), F32),
            dma((3,)),
            dma((5,)),
            dma((2,)),
            dma((2,)),
            dma((2,)),
            dma((2,)),
            dma((6,)),
            dma((4,)),
            dma((2,)),
            dma((1,)),
            dma((23,)),
        ],
        compiler_params=pltpu.CompilerParams(
            collective_id=0, has_side_effects=True, vmem_limit_bytes=50 * 2**20
        ),
        name="cross_spectra",
    )(source_blocks, band_bins, raw_strain, table())
    return rows.reshape(SHARE, NB, 2, CH).transpose(0, 2, 1, 3).astype(BF16)


def solution(mesh):
    in_specs = (P("tm", "chan"), P(), P())
    out_specs = P("tm", None, None, "chan")
    return jax.shard_map(body, mesh=mesh, in_specs=in_specs, out_specs=out_specs, check_vma=False)
```

```python
import functools
import math

import jax
import jax.numpy as jnp
import numpy as np
from jax import lax
from jax.experimental import pallas as pl
from jax.experimental.pallas import tpu as pltpu
from jax.sharding import PartitionSpec as P

NW = 16
WIN = 500
NB = 20
VS = 640
TAPS = 64
DECIM = 4
CH = 128
ROWS = DECIM * NW * WIN
OUTS = NW * WIN
MB = 112
KB = 512
STEP = DECIM * MB
PAIRS = 36
HALO = 64
RAW_PAD = HALO + 2 * PAIRS * STEP
DEC_PAD = 2 * PAIRS * MB
EB = 256
EN_PAD = 8192
CHUNKS = (0, 6272, 11648, 17024, 22400, 27776, ROWS)
DR = 48
MAIN = 16
AR = 40
SR = 56
QR = 400
SHARE = 160
HR = QR // 2
FAR_FIRST = sorted(
    ((dy, dx) for dy in range(4) for dx in range(4) if dy or dx),
    key=lambda step: (-min(step[0], 4 - step[0]) - min(step[1], 4 - step[1]), step),
)
FR = 104
FORGET = math.exp(-1.0 / WIN)
F32 = jnp.float32
BF16 = jnp.bfloat16
MESH = pl.DeviceIdType.MESH


def lowpass_taps():
    offsets = np.arange(TAPS) - (TAPS - 1) / 2.0
    window = 0.54 - 0.46 * np.cos(2.0 * np.pi * np.arange(TAPS) / (TAPS - 1))
    angles = np.pi * 0.8 * offsets / DECIM
    values = np.sin(angles) / angles * window
    return values / values.sum()


def make_tables(table_v, filter_v, within_v):
    taps = lowpass_taps().astype(jnp.bfloat16).astype(np.float32)
    row = lax.broadcasted_iota(jnp.int32, (8, CH), 0)
    lane = lax.broadcasted_iota(jnp.int32, (8, CH), 1)
    lag = DECIM * row + DECIM - 1 + HALO - lane
    eight = jnp.zeros((8, CH), F32)
    for j in range(TAPS):
        eight = jnp.where(lag == j, float(taps[j]), eight)
    for b in range(MB // 16):
        rows = []
        for half in range(2):
            shift = 32 * (2 * b + half)
            turned = pltpu.roll(eight, shift % CH, axis=1) if shift % CH else eight
            columns = []
            for q in range(KB // CH):
                if q == shift // CH:
                    columns.append(jnp.where(lane >= shift % CH, turned, 0.0))
                elif q == shift // CH + 1:
                    columns.append(jnp.where(lane < shift % CH, turned, 0.0))
                else:
                    columns.append(jnp.zeros((8, CH), F32))
            rows.append(jnp.concatenate(columns, axis=1))
        filter_v[16 * b : 16 * b + 16, :] = jnp.concatenate(rows, axis=0).astype(BF16)
    gap = lax.broadcasted_iota(jnp.int32, (EB, EB), 0) - lax.broadcasted_iota(jnp.int32, (EB, EB), 1)
    share = (1.0 - FORGET) * jnp.exp(jnp.maximum(gap, 0).astype(F32) * (-1.0 / WIN))
    within_v[...] = jnp.where(gap >= 0, share, 0.0).astype(BF16)
    row = lax.broadcasted_iota(jnp.int32, (DR, 512), 0)
    time = lax.broadcasted_iota(jnp.int32, (DR, 512), 1)
    late = row >= 2 * MAIN
    bin_id = jnp.where(late, MAIN + row % 4, row % MAIN)
    quarter = jnp.where(late, row // 4 % 2, row // MAIN % 2)
    angle = ((bin_id + 1) * time + (WIN // 4) * quarter).astype(F32)
    angle = angle - jnp.floor(angle * (1.0 / WIN)) * WIN
    angle = jnp.where(angle < 0.0, angle + WIN, jnp.where(angle >= WIN, angle - WIN, angle))
    angle = jnp.minimum(angle, WIN - angle)
    flip = angle > WIN / 4.0
    angle = jnp.where(flip, WIN / 2.0 - angle, angle)
    square = (angle * angle) * ((2.0 * math.pi / WIN) ** 2)
    cosine = jnp.full((DR, 512), 1.0, F32)
    for order in (14, 12, 10, 8, 6, 4, 2):
        cosine = 1.0 - square * cosine * (1.0 / (order * (order - 1)))
    cosine = jnp.where(flip, -cosine, cosine) * (1.0 / math.sqrt(WIN))
    cosine = jnp.where((time < WIN) & (row < 2 * NB), cosine, 0.0)
    for place in range(4):
        shifted = pltpu.roll(cosine, 4 * place, axis=1) if place else cosine
        table_v[place] = shifted.astype(BF16)


def kernel(
    blocks_hbm, band_hbm, raw_ref, out_ref,
    blocks_ref, band_ref, table_v, filter_v, within_v, raw_v, dec_v, en_v, run_v, norm_v, white_v, total_v, totals_v,
    own_v, first_v, share_v, shares_v, rows_v, pieces_v, rising_v, weights_v,
    small_sem, raw_sem, halo_sem, tot_sem, a_sem, b_sem, own_ssem, own_rsem, hand_sem, q_ssem, q_rsem,
):
    tm = lax.axis_index("tm")
    chan = lax.axis_index("chan")
    zl, core = tm // 2, tm % 2
    zh, pid = chan // 16, chan % 16
    y, x = pid // 4, pid % 4
    line = zh * 8 + tm
    totals_v[...] = jnp.zeros(totals_v.shape, F32)

    def repeat(count, step):
        lax.fori_loop(0, count, lambda n, carry: (step(n), carry)[1], 0)

    def unrolled(count, step):
        for n in range(count):
            step(n)

    def plane_device(other):
        return (tm, zh * 16 + other)

    def line_device(other):
        return (other % 8, (other // 8) * 16 + pid)

    barrier = pltpu.get_barrier_semaphore()

    def greet(n):
        pl.semaphore_signal(
            barrier, inc=1, device_id=line_device((line + n + 1) % 16), device_id_type=MESH
        )
        pl.semaphore_signal(
            barrier, inc=1, device_id=plane_device((pid + n + 1) % 16), device_id_type=MESH
        )

    repeat(15, greet)

    def chunk(c):
        first, last = CHUNKS[c], CHUNKS[c + 1]
        return pltpu.make_async_copy(
            raw_ref.at[pl.ds(first, last - first)],
            raw_v.at[pl.ds(HALO + first, last - first)],
            raw_sem.at[c],
        )

    small = [
        pltpu.make_async_copy(source, target, small_sem.at[n])
        for n, (source, target) in enumerate(
            ((blocks_hbm, blocks_ref), (band_hbm, band_ref))
        )
    ]
    for c in range(6):
        chunk(c).start()
    small[0].start()
    small[1].start()
    raw_v[HALO + ROWS : RAW_PAD, :] = jnp.zeros((RAW_PAD - HALO - ROWS, CH), BF16)
    en_v[DEC_PAD:EN_PAD, :] = jnp.zeros((EN_PAD - DEC_PAD, CH), BF16)
    dec_v[DEC_PAD:EN_PAD, :] = jnp.zeros((EN_PAD - DEC_PAD, CH), F32)

    @pl.when(tm == 0)
    def _():
        raw_v[0:HALO, :] = jnp.zeros((HALO, CH), BF16)

    def halo_to(other):
        return pltpu.make_async_remote_copy(
            src_ref=raw_ref.at[pl.ds(ROWS - HALO, HALO)],
            dst_ref=raw_v.at[pl.ds(0, HALO)],
            send_sem=halo_sem.at[0],
            recv_sem=halo_sem.at[1],
            device_id=(other, chan),
            device_id_type=MESH,
        )

    tail = OUTS - (2 * PAIRS - 1) * MB
    back = lax.broadcasted_iota(jnp.int32, (MB, CH), 0).astype(F32) - (MB - 1.0)
    weights_v[0] = (1.0 - FORGET) * jnp.exp(back * (1.0 / WIN))
    back = back + float(MB - tail)
    weights_v[1] = jnp.where(
        back <= 0.0, (1.0 - FORGET) * jnp.exp(jnp.minimum(back, 0.0) * (1.0 / WIN)), 0.0
    )
    place = lax.broadcasted_iota(jnp.int32, (EB, CH), 0).astype(F32)
    rising_v[...] = jnp.exp((place + 1.0) * (-1.0 / WIN))
    make_tables(table_v, filter_v, within_v)

    block_fade = FORGET**MB
    tail_fade = FORGET**tail

    def decimate(n, total):
        pair = (n + 1) % PAIRS
        is_tail, is_first = pair == PAIRS - 1, pair == 0
        start = pl.multiple_of(pair * (2 * STEP), 128)
        left = raw_v[pl.ds(start, KB), :]
        right = raw_v[pl.ds(start + STEP, KB), :]
        both = jnp.dot(
            filter_v[...], jnp.concatenate([left, right], axis=1), preferred_element_type=F32
        )
        row = pl.multiple_of(pair * (2 * MB), 32)
        sums = []
        for half in range(2):
            values = both[:, half * CH : (half + 1) * CH]
            dec_v[pl.ds(row + half * MB, MB), :] = values
            energy = values * values
            en_v[pl.ds(row + half * MB, MB), :] = energy.astype(BF16)
            weights = weights_v[0] if half == 0 else weights_v[pair // (PAIRS - 1)]
            sums.append(jnp.sum((weights * energy).reshape(MB // 8, 8, CH), axis=0))
        fade = jnp.where(is_tail, tail_fade, block_fade).astype(F32)
        decay = jnp.where(is_first, 1.0, block_fade * fade).astype(F32)
        gain = jnp.where(is_first, FORGET ** (OUTS - 2 * MB), 1.0).astype(F32)
        return total * decay + (sums[0] * fade + sums[1]) * gain

    def two_pairs(n, total):
        return decimate(n + 1, decimate(n, total))

    def stretch(c, total):
        for n in range(6):

            @pl.when(c == n)
            def _():
                chunk(n).wait()

        @pl.when(c == 4)
        def _():
            pl.semaphore_wait(barrier, 30)

            @pl.when(tm < 7)
            def _():
                halo_to(tm + 1).start()

        @pl.when((c == 5) & (tm > 0))
        def _():
            halo_to(tm - 1).wait_recv()

        return lax.fori_loop(0, 3, lambda n, t: two_pairs(6 * c + 2 * n, t), total)

    total = lax.fori_loop(0, 6, stretch, jnp.zeros((8, CH), F32))
    total_v[...] = jnp.broadcast_to(jnp.sum(total, axis=0, keepdims=True), (8, CH))

    def total_to(other):
        return pltpu.make_async_remote_copy(
            src_ref=total_v,
            dst_ref=totals_v.at[tm],
            send_sem=tot_sem.at[0],
            recv_sem=tot_sem.at[1],
            device_id=(other, chan),
            device_id_type=MESH,
        )

    repeat(7, lambda n: total_to((tm + n + 1) % 8).start())

    def arrived(ref, sem):
        pltpu.make_async_remote_copy(
            src_ref=ref, dst_ref=ref, send_sem=sem, recv_sem=sem,
            device_id=plane_device((pid + 1) % 16), device_id_type=MESH,
        ).wait_recv()

    def departed(ref, sem):
        pltpu.make_async_remote_copy(
            src_ref=ref, dst_ref=ref, send_sem=sem, recv_sem=sem,
            device_id=plane_device((pid + 1) % 16), device_id_type=MESH,
        ).wait_send()

    def local_run(n):
        row = pl.multiple_of(n * (2 * EB), 2 * EB)
        rhs = jnp.concatenate([en_v[pl.ds(row, EB), :], en_v[pl.ds(row + EB, EB), :]], axis=1)
        both = jnp.dot(within_v[...], rhs, preferred_element_type=F32)
        run_v[pl.ds(row, EB), :] = both[:, :CH]
        run_v[pl.ds(row + EB, EB), :] = both[:, CH:]

    repeat(EN_PAD // (2 * EB), local_run)
    arrived(totals_v.at[pl.ds(0, 7)], tot_sem.at[1])

    state = jnp.zeros((8, CH), F32)
    for group in range(7):
        state = jnp.where(group < tm, state * math.exp(-NW) + totals_v[group], state)

    def normalize(block, state):
        row = pl.multiple_of(block * EB, EB)
        running = run_v[pl.ds(row, EB), :] + rising_v[...] * state[0:1, :]
        values = dec_v[pl.ds(row, EB), :] * lax.rsqrt(jnp.maximum(running, 0.01))
        norm_v[pl.ds(row, EB), :] = values.astype(BF16)
        return jnp.broadcast_to(running[EB - 1 : EB, :], (8, CH))

    lax.fori_loop(0, OUTS // EB + 1, normalize, state)

    small[0].wait()
    small[1].wait()
    low, high = band_ref[0], band_ref[1]
    row_id = lax.broadcasted_iota(jnp.int32, (2 * NB, CH), 0)
    bin_id = jnp.where(row_id < 2 * MAIN, row_id % MAIN, MAIN + row_id % 4)
    keep = jnp.where((bin_id >= low) & (bin_id < high), 1.0, 0.0).astype(F32)

    def spectra_of(n):
        first = n + n // 4 * 4
        start = first * WIN // 16 * 16
        rhs = jnp.concatenate(
            [norm_v[pl.ds(start, 512), :], norm_v[pl.ds(start + 4 * WIN, 512), :]], axis=1
        )
        both = jnp.dot(table_v[first * WIN % 16 // 4], rhs, preferred_element_type=F32)
        for half in range(2):
            w = first + 4 * half
            spectra = both[: 2 * NB, half * CH : (half + 1) * CH]
            power = jnp.sum(spectra * spectra, axis=0, keepdims=True) / NB
            white = spectra * keep * lax.rsqrt(jnp.maximum(power, 0.1))
            for p in range(2):
                white_v[pl.ds(p * NW + w, MAIN, stride=AR), :] = white[p * MAIN : (p + 1) * MAIN]
                white_v[pl.ds(w // 4 * (4 * AR) + 32 + p * 4 + w % 4, 4, stride=AR), :] = white[
                    32 + 4 * p : 36 + 4 * p
                ]

    unrolled(8, spectra_of)
    own_v[tm] = white_v[...].reshape(MAIN, AR, CH).astype(BF16)

    def plane_copy(other):
        return pltpu.make_async_remote_copy(
            src_ref=own_v.at[tm, other],
            dst_ref=first_v.at[pid],
            send_sem=a_sem.at[0],
            recv_sem=a_sem.at[1],
            device_id=plane_device(other),
            device_id_type=MESH,
        )

    for dy, dx in FAR_FIRST:
        plane_copy((y + dy) % 4 * 4 + (x + dx) % 4).start()

    def own_copy(group, other, slot, arrival):
        return pltpu.make_async_remote_copy(
            src_ref=own_v.at[group],
            dst_ref=own_v.at[group],
            send_sem=own_ssem.at[slot],
            recv_sem=arrival,
            device_id=(other, chan),
            device_id_type=MESH,
        )

    partner = zl * 2 + 1 - core

    def hand_over(group):
        return pltpu.make_async_remote_copy(
            src_ref=own_v.at[group],
            dst_ref=own_v.at[group],
            send_sem=hand_sem.at[0],
            recv_sem=hand_sem.at[1],
            device_id=(partner, chan),
            device_id_type=MESH,
        )

    sends = []

    def send_along(condition, group, other, slot):
        sends.append((condition, group, other, slot))

        @pl.when(condition)
        def _():
            own_copy(group, other, slot, own_rsem.at[group // 2]).start()

    send_along(zl < 3, tm, tm + 2, 0)
    send_along(zl > 0, tm, tm - 2, 1)
    hand_over(tm).start()

    def relay_own(step):
        below, above = tm - 2 * step, tm + 2 * step

        @pl.when(zl - step >= 0)
        def _():
            own_copy(below, partner, 0, own_rsem.at[below // 2]).wait_recv()

        @pl.when(zl + step <= 3)
        def _():
            own_copy(above, partner, 0, own_rsem.at[above // 2]).wait_recv()

        if step < 3:
            send_along((zl - step >= 0) & (zl < 3), below, tm + 2, 2 * step)
            send_along((zl + step <= 3) & (zl > 0), above, tm - 2, 2 * step + 1)

        @pl.when(zl - step >= 0)
        def _():
            hand_over(below).start()

        @pl.when(zl + step <= 3)
        def _():
            hand_over(above).start()

    first_v[pid] = own_v[tm, pid]
    arrived(first_v.at[pl.ds(0, 15)], a_sem.at[1])

    lane8 = lax.broadcasted_iota(jnp.int32, (8, CH), 1)
    lane40 = lax.broadcasted_iota(jnp.int32, (AR, CH), 1)

    def turn_left(rows, lanes):
        return pltpu.roll(rows, CH - lanes, axis=1) if lanes else rows

    picked = []
    for b in range(2):
        for i in range(5):
            block = blocks_ref[b] + i
            here = jnp.where(block // 16 == zh, 1.0, 0.0).astype(F32)
            picked.append(first_v[block % 16].astype(F32) * here)
    for share in range(8):
        jj = share % 4
        a, c = picked[share // 4 * 5 + jj], picked[share // 4 * 5 + jj + 1]
        turned = turn_left(c, 32 * jj)
        head = jnp.where(lane40 < CH - 32 * jj, turn_left(a, 32 * jj), turned)
        rest = jnp.where(lane8 < 32, turned[0:8], 0.0)
        for q in range(1, 4):
            part = pltpu.roll(turned[8 * q : 8 * q + 8], 32 * q, axis=1)
            rest = jnp.where((lane8 >= 32 * q) & (lane8 < 32 * q + 32), part, rest)
        last_rest = jnp.where(lane8 < 32, turned[32:40], 0.0)
        share_v[share] = jnp.concatenate([head, rest, last_rest], axis=0).astype(BF16)

    def line_copy(other):
        return pltpu.make_async_remote_copy(
            src_ref=share_v.at[other % 8],
            dst_ref=shares_v.at[line],
            send_sem=b_sem.at[0],
            recv_sem=b_sem.at[1],
            device_id=line_device(other),
            device_id_type=MESH,
        )

    for dz in (4, 3, 5, 2, 6, 1, 7):
        for dc in range(2):
            line_copy((line // 2 + dz) % 8 * 2 + (core + dc) % 2).start()
    line_copy(line + 1 - 2 * core).start()
    shares_v[line] = share_v[tm]
    relay_own(1)
    arrived(shares_v.at[pl.ds(0, 15)], b_sem.at[1])

    def unpack(g):
        both = shares_v[g].astype(F32) + shares_v[8 + g].astype(F32)
        rests = [both[40:48]]
        for q in range(1, 4):
            rests.append(pltpu.roll(both[40:48], CH - 32 * q, axis=1))
        rests.append(both[48:56])
        rows = jnp.concatenate([both[0:40], jnp.concatenate(rests, axis=0)], axis=1)
        rows_v[pl.ds(pl.multiple_of(g * 32, 32), 32), :] = rows[0:32]
        rows_v[pl.ds(pl.multiple_of(256 + g * 8, 8), 8), :] = rows[32:40]
        rows_v[pl.ds(pl.multiple_of(320 + g * 8, 8), 8), :] = rows[32:40]

    unrolled(8, unpack)
    eye = (
        lax.broadcasted_iota(jnp.int32, (SHARE, 256), 0)
        == lax.broadcasted_iota(jnp.int32, (SHARE, 256), 1)
    )
    eye = jnp.where(eye, 1.0, 0.0).astype(BF16)
    turned = lax.dot_general(
        eye, rows_v[...].astype(BF16), (((1,), (1,)), ((), ())), preferred_element_type=F32
    )
    half_lane = lax.broadcasted_iota(jnp.int32, (80, CH), 1) < 64
    packed_tail = jnp.where(half_lane, turned[0:80, 2 * CH :], turned[80:160, 2 * CH :])
    pieces_v[pid] = jnp.concatenate(
        [turned[:, :CH], turned[:, CH : 2 * CH], packed_tail], axis=0
    ).astype(BF16)

    def at(h, f, s):
        dx, dy = f * (1 - h) + s * h, f * h + s * (1 - h)
        return ((y + dy) % 4) * 4 + (x + dx) % 4

    def piece_copy(h, f, s, along, across, first, count, event):
        rows = pl.ds(pl.multiple_of(h * HR + first, 8), count)
        return pltpu.make_async_remote_copy(
            src_ref=pieces_v.at[at(h, f, s), rows],
            dst_ref=pieces_v.at[at(h, f, s), rows],
            send_sem=q_ssem.at[0],
            recv_sem=q_rsem.at[event],
            device_id=plane_device(at(h, along, across)),
            device_id_type=MESH,
        )

    def wait_half(h, f, s, event):
        piece_copy(h, f, s, 1, 0, 0, HR, event).wait_recv()

    def send_across(h, f):
        for t in range(2):
            piece_copy(h, f, 0, 0, 1 + 2 * t, 0, HR, h * 11 + 3 + 2 * f + t).start()

    def forward(h, f, s, along, t, event):
        first, count = ((0, FR), (FR, HR - FR))[t]
        step = 1 + 2 * t
        piece_copy(
            h, f, s, step if along else 0, 0 if along else step, first, count, event
        ).start()

    def own_half(h):
        for t in range(2):
            piece_copy(h, 0, 0, 1 + 2 * t, 0, 0, HR, h * 11 + t).start()

    def near_along(h):
        for t in range(2):
            wait_half(h, 3 - 2 * t, 0, h * 11 + t)
            forward(h, 3 - 2 * t, 0, True, t, h * 11 + 2)
            send_across(h, 3 - 2 * t)

    def near_across(h, f):
        for t in range(2):
            wait_half(h, f, 3 - 2 * t, h * 11 + 3 + 2 * f + t)
            forward(h, f, 3 - 2 * t, False, t, 22)

    def far_along(h):
        wait_half(h, 2, 0, h * 11 + 2)
        send_across(h, 2)

    repeat(2, own_half)
    repeat(2, lambda h: send_across(h, 0))
    repeat(2, near_along)
    repeat(2, lambda h: near_across(h, 0))
    repeat(2, far_along)
    relay_own(2)
    repeat(6, lambda n: near_across(n % 2, n // 2 + 1))
    relay_own(3)
    arrived(own_v.at[pl.ds(0, 4)], hand_sem.at[1])

    scale = 1.0 / math.sqrt(8 * NW)

    def put(k, lhs, rhs):
        both = jnp.dot(lhs, rhs, preferred_element_type=F32) * scale
        out_ref[pl.ds(2 * k, SHARE, stride=2 * NB), :] = both[:, :CH]
        out_ref[pl.ds(2 * k + 1, SHARE, stride=2 * NB), :] = both[:, CH:]

    def main_bin(k):
        lhs = jnp.concatenate([pieces_v[k, 0:SHARE], pieces_v[k, SHARE : 2 * SHARE]], axis=1)
        re, im = [], []
        for g in range(8):
            rows = own_v[g, k, 0:32]
            re.append(rows)
            im.append(rows[16:32])
            im.append(-rows[0:16])
        rhs = jnp.concatenate([jnp.concatenate(re, axis=0), jnp.concatenate(im, axis=0)], axis=1)
        put(k, lhs, rhs)

    def near_bin(n):
        f, s = n % 3, n // 3
        main_bin(at(0, f + f // 2, s + s // 2))

    def far_bin(n):
        late, m = n // 4, n % 4
        main_bin(at(0, 2 * (1 - late) + late * (m + m // 2), m * (1 - late) + 2 * late))

    repeat(9, near_bin)
    arrived(pieces_v.at[pl.ds(0, 4)], q_rsem.at[22])
    repeat(7, far_bin)

    sign = jnp.where(lax.broadcasted_iota(jnp.int32, (8, CH), 0) < 4, 1.0, -1.0).astype(F32)

    def tail_bin(kk):
        columns = []
        for pair in range(2):
            even = pieces_v[pair * 8 + kk, 2 * SHARE : QR].astype(F32)
            odd = pieces_v[pair * 8 + 4 + kk, 2 * SHARE : QR].astype(F32)
            upper = jnp.where(half_lane, even, pltpu.roll(odd, 64, axis=1))
            lower = jnp.where(half_lane, pltpu.roll(even, 64, axis=1), odd)
            columns.append(jnp.concatenate([upper, lower], axis=0))
        lhs = jnp.concatenate(columns, axis=1).astype(BF16)
        re, im = [], []
        for wh in range(4):
            for g in range(8):
                rows = own_v[g, wh * 4 + kk, 32:40].astype(F32)
                re.append(rows)
                im.append(pltpu.roll(rows, 4, axis=0) * sign)
        rhs = jnp.concatenate([jnp.concatenate(re, axis=0), jnp.concatenate(im, axis=0)], axis=1)
        put(MAIN + kk, lhs, rhs.astype(BF16))

    repeat(NB - MAIN, tail_bin)

    @pl.when(tm < 7)
    def _():
        halo_to(tm + 1).wait_send()

    departed(totals_v.at[pl.ds(0, 7)], tot_sem.at[0])
    departed(first_v.at[pl.ds(0, 15)], a_sem.at[0])
    departed(shares_v.at[pl.ds(0, 15)], b_sem.at[0])
    departed(own_v.at[pl.ds(0, 4)], hand_sem.at[0])
    departed(pieces_v.at[pl.ds(0, 15)], q_ssem.at[0])
    for condition, group, other, slot in sends:

        @pl.when(condition)
        def _():
            own_copy(group, other, slot, own_rsem.at[0]).wait_send()


def body(raw_strain, source_blocks, band_bins):
    hbm = pl.BlockSpec(memory_space=pltpu.HBM)
    vmem = pl.BlockSpec(memory_space=pltpu.VMEM)
    dma = pltpu.SemaphoreType.DMA
    rows = pl.pallas_call(
        kernel,
        out_shape=jax.ShapeDtypeStruct((SHARE * NB * 2, CH), F32),
        in_specs=[hbm] * 3,
        out_specs=vmem,
        scratch_shapes=[
            pltpu.SMEM((2,), jnp.int32),
            pltpu.SMEM((2,), jnp.int32),
            pltpu.VMEM((4, DR, 512), BF16),
            pltpu.VMEM((MB, KB), BF16),
            pltpu.VMEM((EB, EB), BF16),
            pltpu.VMEM((RAW_PAD, CH), BF16),
            pltpu.VMEM((EN_PAD, CH), F32),
            pltpu.VMEM((EN_PAD, CH), BF16),
            pltpu.VMEM((EN_PAD, CH), F32),
            pltpu.VMEM((EN_PAD, CH), BF16),
            pltpu.VMEM((MAIN * AR, CH), F32),
            pltpu.VMEM((8, CH), F32),
            pltpu.VMEM((8, 8, CH), F32),
            pltpu.VMEM((8, MAIN, AR, CH), BF16),
            pltpu.VMEM((16, AR, CH), BF16),
            pltpu.VMEM((8, SR, CH), BF16),
            pltpu.VMEM((16, SR, CH), BF16),
            pltpu.VMEM((384, 256), F32),
            pltpu.VMEM((16, QR, CH), BF16),
            pltpu.VMEM((EB, CH), F32),
            pltpu.VMEM((2, MB, CH), F32),
            dma((2,)),
            dma((6,)),
            dma((2,)),
            dma((2,)),
            dma((2,)),
            dma((2,)),
            dma((6,)),
            dma((4,)),
            dma((2,)),
            dma((1,)),
            dma((23,)),
        ],
        compiler_params=pltpu.CompilerParams(
            collective_id=0, has_side_effects=True, vmem_limit_bytes=50 * 2**20
        ),
        name="cross_spectra",
    )(source_blocks, band_bins, raw_strain)
    return rows.reshape(SHARE, NB, 2, CH).transpose(0, 2, 1, 3).astype(BF16)


def solution(mesh):
    in_specs = (P("tm", "chan"), P(), P())
    out_specs = P("tm", None, None, "chan")
    return jax.shard_map(body, mesh=mesh, in_specs=in_specs, out_specs=out_specs, check_vma=False)
```

```python
import functools
import math

import jax
import jax.numpy as jnp
import numpy as np
from jax import lax
from jax.experimental import pallas as pl
from jax.experimental.pallas import tpu as pltpu
from jax.sharding import PartitionSpec as P

NW = 16
WIN = 500
NB = 20
VS = 640
TAPS = 64
DECIM = 4
CH = 128
ROWS = DECIM * NW * WIN
OUTS = NW * WIN
MB = 112
KB = 512
STEP = DECIM * MB
PAIRS = 36
HALO = 64
RAW_PAD = HALO + 2 * PAIRS * STEP
DEC_PAD = 2 * PAIRS * MB
EB = 256
EN_PAD = 8192
CHUNKS = (0, 6272, 11648, 17024, 22400, 27776, ROWS)
DR = 48
MAIN = 16
AR = 40
SR = 56
QR = 400
SHARE = 160
HR = QR // 2
FAR_FIRST = sorted(
    ((dy, dx) for dy in range(4) for dx in range(4) if dy or dx),
    key=lambda step: (-min(step[0], 4 - step[0]) - min(step[1], 4 - step[1]), step),
)
FR = 104
FORGET = math.exp(-1.0 / WIN)
F32 = jnp.float32
BF16 = jnp.bfloat16
MESH = pl.DeviceIdType.MESH


def lowpass_taps():
    offsets = np.arange(TAPS) - (TAPS - 1) / 2.0
    window = 0.54 - 0.46 * np.cos(2.0 * np.pi * np.arange(TAPS) / (TAPS - 1))
    angles = np.pi * 0.8 * offsets / DECIM
    values = np.sin(angles) / angles * window
    return values / values.sum()


def make_tables(table_v, filter_v, within_v):
    taps = lowpass_taps().astype(jnp.bfloat16).astype(np.float32)
    row = lax.broadcasted_iota(jnp.int32, (8, CH), 0)
    lane = lax.broadcasted_iota(jnp.int32, (8, CH), 1)
    lag = DECIM * row + DECIM - 1 + HALO - lane
    eight = jnp.zeros((8, CH), F32)
    for j in range(TAPS):
        eight = jnp.where(lag == j, float(taps[j]), eight)
    for b in range(MB // 16):
        rows = []
        for half in range(2):
            shift = 32 * (2 * b + half)
            turned = pltpu.roll(eight, shift % CH, axis=1) if shift % CH else eight
            columns = []
            for q in range(KB // CH):
                if q == shift // CH:
                    columns.append(jnp.where(lane >= shift % CH, turned, 0.0))
                elif q == shift // CH + 1:
                    columns.append(jnp.where(lane < shift % CH, turned, 0.0))
                else:
                    columns.append(jnp.zeros((8, CH), F32))
            rows.append(jnp.concatenate(columns, axis=1))
        filter_v[16 * b : 16 * b + 16, :] = jnp.concatenate(rows, axis=0).astype(BF16)
    gap = lax.broadcasted_iota(jnp.int32, (EB, EB), 0) - lax.broadcasted_iota(jnp.int32, (EB, EB), 1)
    share = (1.0 - FORGET) * jnp.exp(jnp.maximum(gap, 0).astype(F32) * (-1.0 / WIN))
    within_v[...] = jnp.where(gap >= 0, share, 0.0).astype(BF16)
    row = lax.broadcasted_iota(jnp.int32, (DR, 512), 0)
    time = lax.broadcasted_iota(jnp.int32, (DR, 512), 1)
    late = row >= 2 * MAIN
    bin_id = jnp.where(late, MAIN + row % 4, row % MAIN)
    quarter = jnp.where(late, row // 4 % 2, row // MAIN % 2)
    angle = ((bin_id + 1) * time + (WIN // 4) * quarter).astype(F32)
    angle = angle - jnp.floor(angle * (1.0 / WIN)) * WIN
    angle = jnp.where(angle < 0.0, angle + WIN, jnp.where(angle >= WIN, angle - WIN, angle))
    angle = jnp.minimum(angle, WIN - angle)
    flip = angle > WIN / 4.0
    angle = jnp.where(flip, WIN / 2.0 - angle, angle)
    square = (angle * angle) * ((2.0 * math.pi / WIN) ** 2)
    cosine = jnp.full((DR, 512), 1.0, F32)
    for order in (14, 12, 10, 8, 6, 4, 2):
        cosine = 1.0 - square * cosine * (1.0 / (order * (order - 1)))
    cosine = jnp.where(flip, -cosine, cosine) * (1.0 / math.sqrt(WIN))
    cosine = jnp.where((time < WIN) & (row < 2 * NB), cosine, 0.0)
    for place in range(4):
        shifted = pltpu.roll(cosine, 4 * place, axis=1) if place else cosine
        table_v[place] = shifted.astype(BF16)


def kernel(
    small_hbm, raw_ref, out_ref,
    blocks_ref, table_v, filter_v, within_v, raw_v, dec_v, en_v, run_v, norm_v, white_v, total_v, totals_v,
    own_v, first_v, share_v, shares_v, rows_v, pieces_v, rising_v, weights_v,
    small_sem, raw_sem, halo_sem, tot_ssem, tot_rsem, a_sem, b_sem, own_ssem, own_rsem, hand_sem, q_ssem, q_rsem,
):
    tm = lax.axis_index("tm")
    chan = lax.axis_index("chan")
    zl, core = tm // 2, tm % 2
    zh, pid = chan // 16, chan % 16
    y, x = pid // 4, pid % 4
    line = zh * 8 + tm
    totals_v[...] = jnp.zeros(totals_v.shape, F32)

    def repeat(count, step):
        lax.fori_loop(0, count, lambda n, carry: (step(n), carry)[1], 0)

    def unrolled(count, step):
        for n in range(count):
            step(n)

    def plane_device(other):
        return (tm, zh * 16 + other)

    def line_device(other):
        return (other % 8, (other // 8) * 16 + pid)

    def chunk(c):
        first, last = CHUNKS[c], CHUNKS[c + 1]
        return pltpu.make_async_copy(
            raw_ref.at[pl.ds(first, last - first)],
            raw_v.at[pl.ds(HALO + first, last - first)],
            raw_sem.at[c],
        )

    small = [
        pltpu.make_async_copy(source, target, small_sem.at[n])
        for n, (source, target) in enumerate(
            ((small_hbm, blocks_ref),)
        )
    ]
    for c in range(6):
        chunk(c).start()
    small[0].start()

    barrier = pltpu.get_barrier_semaphore()

    def greet(n):
        pl.semaphore_signal(
            barrier, inc=1, device_id=line_device((line + n + 1) % 16), device_id_type=MESH
        )
        pl.semaphore_signal(
            barrier, inc=1, device_id=plane_device((pid + n + 1) % 16), device_id_type=MESH
        )

    repeat(15, greet)

    raw_v[HALO + ROWS : RAW_PAD, :] = jnp.zeros((RAW_PAD - HALO - ROWS, CH), BF16)
    en_v[DEC_PAD:EN_PAD, :] = jnp.zeros((EN_PAD - DEC_PAD, CH), BF16)
    dec_v[DEC_PAD:EN_PAD, :] = jnp.zeros((EN_PAD - DEC_PAD, CH), F32)

    @pl.when(tm == 0)
    def _():
        raw_v[0:HALO, :] = jnp.zeros((HALO, CH), BF16)

    def halo_to(other):
        return pltpu.make_async_remote_copy(
            src_ref=raw_ref.at[pl.ds(ROWS - HALO, HALO)],
            dst_ref=raw_v.at[pl.ds(0, HALO)],
            send_sem=halo_sem.at[0],
            recv_sem=halo_sem.at[1],
            device_id=(other, chan),
            device_id_type=MESH,
        )

    tail = OUTS - (2 * PAIRS - 1) * MB
    back = lax.broadcasted_iota(jnp.int32, (MB, CH), 0).astype(F32) - (MB - 1.0)
    weights_v[0] = (1.0 - FORGET) * jnp.exp(back * (1.0 / WIN))
    back = back + float(MB - tail)
    weights_v[1] = jnp.where(
        back <= 0.0, (1.0 - FORGET) * jnp.exp(jnp.minimum(back, 0.0) * (1.0 / WIN)), 0.0
    )
    place = lax.broadcasted_iota(jnp.int32, (EB, CH), 0).astype(F32)
    rising_v[...] = jnp.exp((place + 1.0) * (-1.0 / WIN))
    make_tables(table_v, filter_v, within_v)

    block_fade = FORGET**MB
    tail_fade = FORGET**tail

    def decimate(n, total):
        pair = (n + 1) % PAIRS
        is_tail, is_first = pair == PAIRS - 1, pair == 0
        start = pl.multiple_of(pair * (2 * STEP), 128)
        left = raw_v[pl.ds(start, KB), :]
        right = raw_v[pl.ds(start + STEP, KB), :]
        both = jnp.dot(
            filter_v[...], jnp.concatenate([left, right], axis=1), preferred_element_type=F32
        )
        row = pl.multiple_of(pair * (2 * MB), 32)
        sums = []
        for half in range(2):
            values = both[:, half * CH : (half + 1) * CH]
            dec_v[pl.ds(row + half * MB, MB), :] = values
            energy = values * values
            en_v[pl.ds(row + half * MB, MB), :] = energy.astype(BF16)
            weights = weights_v[0] if half == 0 else weights_v[pair // (PAIRS - 1)]
            sums.append(jnp.sum((weights * energy).reshape(MB // 8, 8, CH), axis=0))
        fade = jnp.where(is_tail, tail_fade, block_fade).astype(F32)
        decay = jnp.where(is_first, 1.0, block_fade * fade).astype(F32)
        gain = jnp.where(is_first, FORGET ** (OUTS - 2 * MB), 1.0).astype(F32)
        return total * decay + (sums[0] * fade + sums[1]) * gain

    def two_pairs(n, total):
        return decimate(n + 1, decimate(n, total))

    def stretch(c, total):
        for n in range(6):

            @pl.when(c == n)
            def _():
                chunk(n).wait()

        @pl.when(c == 4)
        def _():
            pl.semaphore_wait(barrier, 30)

            @pl.when(tm < 7)
            def _():
                halo_to(tm + 1).start()

        @pl.when((c == 5) & (tm > 0))
        def _():
            halo_to(tm - 1).wait_recv()

        return lax.fori_loop(0, 3, lambda n, t: two_pairs(6 * c + 2 * n, t), total)

    total = lax.fori_loop(0, 6, stretch, jnp.zeros((8, CH), F32))
    total_v[...] = jnp.broadcast_to(jnp.sum(total, axis=0, keepdims=True), (8, CH))

    def total_to(other, group, slot):
        return pltpu.make_async_remote_copy(
            src_ref=total_v,
            dst_ref=totals_v.at[group],
            send_sem=tot_ssem.at[slot],
            recv_sem=tot_rsem.at[group],
            device_id=(other, chan),
            device_id_type=MESH,
        )

    def total_sent(n):
        return total_to(tm + 1 + n, tm, n)

    lax.fori_loop(0, 7 - tm, lambda n, carry: (total_sent(n).start(), carry)[1], 0)

    def arrived(ref, sem):
        pltpu.make_async_remote_copy(
            src_ref=ref, dst_ref=ref, send_sem=sem, recv_sem=sem,
            device_id=plane_device((pid + 1) % 16), device_id_type=MESH,
        ).wait_recv()

    def departed(ref, sem):
        pltpu.make_async_remote_copy(
            src_ref=ref, dst_ref=ref, send_sem=sem, recv_sem=sem,
            device_id=plane_device((pid + 1) % 16), device_id_type=MESH,
        ).wait_send()

    def local_run(n):
        row = pl.multiple_of(n * (2 * EB), 2 * EB)
        rhs = jnp.concatenate([en_v[pl.ds(row, EB), :], en_v[pl.ds(row + EB, EB), :]], axis=1)
        both = jnp.dot(within_v[...], rhs, preferred_element_type=F32)
        run_v[pl.ds(row, EB), :] = both[:, :CH]
        run_v[pl.ds(row + EB, EB), :] = both[:, CH:]

    repeat(EN_PAD // (4 * EB), lambda n: (local_run(2 * n), local_run(2 * n + 1)))

    def total_taken(group, carry):
        total_to((tm + 1) % 8, group, 0).wait_recv()
        return carry

    lax.fori_loop(0, tm, total_taken, 0)

    state = jnp.zeros((8, CH), F32)
    for group in range(7):
        state = jnp.where(group < tm, state * math.exp(-NW) + totals_v[group], state)

    def normalize(block, state):
        row = pl.multiple_of(block * EB, EB)
        running = run_v[pl.ds(row, EB), :] + rising_v[...] * state[0:1, :]
        values = dec_v[pl.ds(row, EB), :] * lax.rsqrt(jnp.maximum(running, 0.01))
        norm_v[pl.ds(row, EB), :] = values.astype(BF16)
        return jnp.broadcast_to(running[EB - 1 : EB, :], (8, CH))

    lax.fori_loop(
        0, EN_PAD // (2 * EB), lambda n, s: normalize(2 * n + 1, normalize(2 * n, s)), state
    )

    small[0].wait()
    low, high = blocks_ref[2], blocks_ref[3]
    row_id = lax.broadcasted_iota(jnp.int32, (2 * NB, CH), 0)
    bin_id = jnp.where(row_id < 2 * MAIN, row_id % MAIN, MAIN + row_id % 4)
    keep = jnp.where((bin_id >= low) & (bin_id < high), 1.0, 0.0).astype(F32)

    def spectra_of(n):
        first = n + n // 4 * 4
        start = first * WIN // 16 * 16
        rhs = jnp.concatenate(
            [norm_v[pl.ds(start, 512), :], norm_v[pl.ds(start + 4 * WIN, 512), :]], axis=1
        )
        both = jnp.dot(table_v[first * WIN % 16 // 4], rhs, preferred_element_type=F32)
        for half in range(2):
            w = first + 4 * half
            spectra = both[: 2 * NB, half * CH : (half + 1) * CH]
            power = jnp.sum(spectra * spectra, axis=0, keepdims=True) / NB
            white = spectra * keep * lax.rsqrt(jnp.maximum(power, 0.1))
            for p in range(2):
                white_v[pl.ds(p * NW + w, MAIN, stride=AR), :] = white[p * MAIN : (p + 1) * MAIN]
                white_v[pl.ds(w // 4 * (4 * AR) + 32 + p * 4 + w % 4, 4, stride=AR), :] = white[
                    32 + 4 * p : 36 + 4 * p
                ]

    unrolled(8, spectra_of)
    own_v[tm] = white_v[...].reshape(MAIN, AR, CH).astype(BF16)

    def plane_copy(other):
        return pltpu.make_async_remote_copy(
            src_ref=own_v.at[tm, other],
            dst_ref=first_v.at[pid],
            send_sem=a_sem.at[0],
            recv_sem=a_sem.at[1],
            device_id=plane_device(other),
            device_id_type=MESH,
        )

    for dy, dx in FAR_FIRST:
        plane_copy((y + dy) % 4 * 4 + (x + dx) % 4).start()

    def own_copy(group, other, slot, arrival):
        return pltpu.make_async_remote_copy(
            src_ref=own_v.at[group],
            dst_ref=own_v.at[group],
            send_sem=own_ssem.at[slot],
            recv_sem=arrival,
            device_id=(other, chan),
            device_id_type=MESH,
        )

    partner = zl * 2 + 1 - core

    def hand_over(group):
        return pltpu.make_async_remote_copy(
            src_ref=own_v.at[group],
            dst_ref=own_v.at[group],
            send_sem=hand_sem.at[0],
            recv_sem=hand_sem.at[1],
            device_id=(partner, chan),
            device_id_type=MESH,
        )

    sends = []

    def send_along(condition, group, other, slot):
        sends.append((condition, group, other, slot))

        @pl.when(condition)
        def _():
            own_copy(group, other, slot, own_rsem.at[group // 2]).start()

    send_along(zl < 3, tm, tm + 2, 0)
    send_along(zl > 0, tm, tm - 2, 1)
    hand_over(tm).start()

    def relay_own(step):
        below, above = tm - 2 * step, tm + 2 * step

        @pl.when(zl - step >= 0)
        def _():
            own_copy(below, partner, 0, own_rsem.at[below // 2]).wait_recv()

        @pl.when(zl + step <= 3)
        def _():
            own_copy(above, partner, 0, own_rsem.at[above // 2]).wait_recv()

        if step < 3:
            send_along((zl - step >= 0) & (zl < 3), below, tm + 2, 2 * step)
            send_along((zl + step <= 3) & (zl > 0), above, tm - 2, 2 * step + 1)

        @pl.when(zl - step >= 0)
        def _():
            hand_over(below).start()

        @pl.when(zl + step <= 3)
        def _():
            hand_over(above).start()

    first_v[pid] = own_v[tm, pid]
    arrived(first_v.at[pl.ds(0, 15)], a_sem.at[1])

    lane8 = lax.broadcasted_iota(jnp.int32, (8, CH), 1)
    lane40 = lax.broadcasted_iota(jnp.int32, (AR, CH), 1)

    def turn_left(rows, lanes):
        return pltpu.roll(rows, CH - lanes, axis=1) if lanes else rows

    picked = []
    for b in range(2):
        for i in range(5):
            block = blocks_ref[b] + i
            here = jnp.where(block // 16 == zh, 1.0, 0.0).astype(F32)
            picked.append(first_v[block % 16].astype(F32) * here)
    for share in range(8):
        jj = share % 4
        a, c = picked[share // 4 * 5 + jj], picked[share // 4 * 5 + jj + 1]
        turned = turn_left(c, 32 * jj)
        head = jnp.where(lane40 < CH - 32 * jj, turn_left(a, 32 * jj), turned)
        rest = jnp.where(lane8 < 32, turned[0:8], 0.0)
        for q in range(1, 4):
            part = pltpu.roll(turned[8 * q : 8 * q + 8], 32 * q, axis=1)
            rest = jnp.where((lane8 >= 32 * q) & (lane8 < 32 * q + 32), part, rest)
        last_rest = jnp.where(lane8 < 32, turned[32:40], 0.0)
        share_v[share] = jnp.concatenate([head, rest, last_rest], axis=0).astype(BF16)

    def line_copy(other):
        return pltpu.make_async_remote_copy(
            src_ref=share_v.at[other % 8],
            dst_ref=shares_v.at[line],
            send_sem=b_sem.at[0],
            recv_sem=b_sem.at[1],
            device_id=line_device(other),
            device_id_type=MESH,
        )

    for dz in (4, 3, 5, 2, 6, 1, 7):
        for dc in range(2):
            line_copy((line // 2 + dz) % 8 * 2 + (core + dc) % 2).start()
    line_copy(line + 1 - 2 * core).start()
    shares_v[line] = share_v[tm]
    relay_own(1)
    arrived(shares_v.at[pl.ds(0, 15)], b_sem.at[1])

    def unpack(g):
        both = shares_v[g].astype(F32) + shares_v[8 + g].astype(F32)
        rests = [both[40:48]]
        for q in range(1, 4):
            rests.append(pltpu.roll(both[40:48], CH - 32 * q, axis=1))
        rests.append(both[48:56])
        rows = jnp.concatenate([both[0:40], jnp.concatenate(rests, axis=0)], axis=1)
        rows_v[pl.ds(pl.multiple_of(g * 32, 32), 32), :] = rows[0:32]
        rows_v[pl.ds(pl.multiple_of(256 + g * 8, 8), 8), :] = rows[32:40]
        rows_v[pl.ds(pl.multiple_of(320 + g * 8, 8), 8), :] = rows[32:40]

    unrolled(8, unpack)
    eye = (
        lax.broadcasted_iota(jnp.int32, (SHARE, 256), 0)
        == lax.broadcasted_iota(jnp.int32, (SHARE, 256), 1)
    )
    eye = jnp.where(eye, 1.0, 0.0).astype(BF16)
    turned = lax.dot_general(
        eye, rows_v[...].astype(BF16), (((1,), (1,)), ((), ())), preferred_element_type=F32
    )
    half_lane = lax.broadcasted_iota(jnp.int32, (80, CH), 1) < 64
    packed_tail = jnp.where(half_lane, turned[0:80, 2 * CH :], turned[80:160, 2 * CH :])
    pieces_v[pid] = jnp.concatenate(
        [turned[:, :CH], turned[:, CH : 2 * CH], packed_tail], axis=0
    ).astype(BF16)

    def at(h, f, s):
        dx, dy = f * (1 - h) + s * h, f * h + s * (1 - h)
        return ((y + dy) % 4) * 4 + (x + dx) % 4

    def piece_copy(h, f, s, along, across, first, count, event):
        rows = pl.ds(pl.multiple_of(h * HR + first, 8), count)
        return pltpu.make_async_remote_copy(
            src_ref=pieces_v.at[at(h, f, s), rows],
            dst_ref=pieces_v.at[at(h, f, s), rows],
            send_sem=q_ssem.at[0],
            recv_sem=q_rsem.at[event],
            device_id=plane_device(at(h, along, across)),
            device_id_type=MESH,
        )

    def wait_half(h, f, s, event):
        piece_copy(h, f, s, 1, 0, 0, HR, event).wait_recv()

    def send_across(h, f):
        for t in range(2):
            piece_copy(h, f, 0, 0, 1 + 2 * t, 0, HR, h * 11 + 3 + 2 * f + t).start()

    def forward(h, f, s, along, t, event):
        first, count = ((0, FR), (FR, HR - FR))[t]
        step = 1 + 2 * t
        piece_copy(
            h, f, s, step if along else 0, 0 if along else step, first, count, event
        ).start()

    def own_half(h):
        for t in range(2):
            piece_copy(h, 0, 0, 1 + 2 * t, 0, 0, HR, h * 11 + t).start()

    def near_along(h):
        for t in range(2):
            wait_half(h, 3 - 2 * t, 0, h * 11 + t)
            forward(h, 3 - 2 * t, 0, True, t, h * 11 + 2)

    def near_spread(h):
        send_across(h, 3)
        send_across(h, 1)

    def near_across(h, f):
        for t in range(2):
            wait_half(h, f, 3 - 2 * t, h * 11 + 3 + 2 * f + t)
            forward(h, f, 3 - 2 * t, False, t, 22)

    def far_along(h):
        wait_half(h, 2, 0, h * 11 + 2)
        send_across(h, 2)

    repeat(2, own_half)
    repeat(2, lambda h: send_across(h, 0))
    repeat(2, near_along)
    repeat(2, near_spread)
    relay_own(2)
    repeat(2, lambda h: near_across(h, 0))
    repeat(2, far_along)
    relay_own(3)

    scale = 1.0 / math.sqrt(8 * NW)

    def put(k, lhs, rhs):
        both = jnp.dot(lhs, rhs, preferred_element_type=F32) * scale
        out_ref[pl.ds(2 * k, SHARE, stride=2 * NB), :] = both[:, :CH]
        out_ref[pl.ds(2 * k + 1, SHARE, stride=2 * NB), :] = both[:, CH:]

    def main_bin(k):
        lhs = jnp.concatenate([pieces_v[k, 0:SHARE], pieces_v[k, SHARE : 2 * SHARE]], axis=1)
        re, im = [], []
        for g in range(8):
            rows = own_v[g, k, 0:32]
            re.append(rows)
            im.append(rows[16:32])
            im.append(-rows[0:16])
        rhs = jnp.concatenate([jnp.concatenate(re, axis=0), jnp.concatenate(im, axis=0)], axis=1)
        put(k, lhs, rhs)

    sign = jnp.where(lax.broadcasted_iota(jnp.int32, (8, CH), 0) < 4, 1.0, -1.0).astype(F32)

    def tail_bin(kk):
        columns = []
        for pair in range(2):
            even = pieces_v[pair * 8 + kk, 2 * SHARE : QR].astype(F32)
            odd = pieces_v[pair * 8 + 4 + kk, 2 * SHARE : QR].astype(F32)
            upper = jnp.where(half_lane, even, pltpu.roll(odd, 64, axis=1))
            lower = jnp.where(half_lane, pltpu.roll(even, 64, axis=1), odd)
            columns.append(jnp.concatenate([upper, lower], axis=0))
        lhs = jnp.concatenate(columns, axis=1).astype(BF16)
        re, im = [], []
        for wh in range(4):
            for g in range(8):
                rows = own_v[g, wh * 4 + kk, 32:40].astype(F32)
                re.append(rows)
                im.append(pltpu.roll(rows, 4, axis=0) * sign)
        rhs = jnp.concatenate([jnp.concatenate(re, axis=0), jnp.concatenate(im, axis=0)], axis=1)
        put(MAIN + kk, lhs, rhs.astype(BF16))

    repeat(2, lambda h: near_across(h, 1))
    arrived(own_v.at[pl.ds(0, 4)], hand_sem.at[1])
    main_bin(pid)
    main_bin(at(0, 1, 0))
    repeat(2, lambda h: near_across(h, 2))
    main_bin(at(0, 3, 0))
    main_bin(at(0, 0, 1))
    repeat(2, lambda h: near_across(h, 3))
    main_bin(at(0, 0, 3))
    for f in (1, 3):
        for s in (1, 3):
            main_bin(at(0, f, s))
    arrived(pieces_v.at[pl.ds(0, 4)], q_rsem.at[22])
    for f, s in ((2, 0), (2, 1), (2, 2), (2, 3), (0, 2), (1, 2), (3, 2)):
        main_bin(at(0, f, s))
    unrolled(NB - MAIN, tail_bin)

    @pl.when(tm < 7)
    def _():
        halo_to(tm + 1).wait_send()

    lax.fori_loop(0, 7 - tm, lambda n, carry: (total_sent(n).wait_send(), carry)[1], 0)
    departed(first_v.at[pl.ds(0, 15)], a_sem.at[0])
    departed(shares_v.at[pl.ds(0, 15)], b_sem.at[0])
    departed(own_v.at[pl.ds(0, 4)], hand_sem.at[0])
    departed(pieces_v.at[pl.ds(0, 15)], q_ssem.at[0])
    for condition, group, other, slot in sends:

        @pl.when(condition)
        def _():
            own_copy(group, other, slot, own_rsem.at[0]).wait_send()


def body(raw_strain, source_blocks, band_bins):
    hbm = pl.BlockSpec(memory_space=pltpu.HBM)
    vmem = pl.BlockSpec(memory_space=pltpu.VMEM)
    dma = pltpu.SemaphoreType.DMA
    rows = pl.pallas_call(
        kernel,
        out_shape=jax.ShapeDtypeStruct((SHARE * NB * 2, CH), F32),
        in_specs=[hbm] * 2,
        out_specs=vmem,
        scratch_shapes=[
            pltpu.SMEM((4,), jnp.int32),
            pltpu.VMEM((4, DR, 512), BF16),
            pltpu.VMEM((MB, KB), BF16),
            pltpu.VMEM((EB, EB), BF16),
            pltpu.VMEM((RAW_PAD, CH), BF16),
            pltpu.VMEM((EN_PAD, CH), F32),
            pltpu.VMEM((EN_PAD, CH), BF16),
            pltpu.VMEM((EN_PAD, CH), F32),
            pltpu.VMEM((EN_PAD, CH), BF16),
            pltpu.VMEM((MAIN * AR, CH), F32),
            pltpu.VMEM((8, CH), F32),
            pltpu.VMEM((8, 8, CH), F32),
            pltpu.VMEM((8, MAIN, AR, CH), BF16),
            pltpu.VMEM((16, AR, CH), BF16),
            pltpu.VMEM((8, SR, CH), BF16),
            pltpu.VMEM((16, SR, CH), BF16),
            pltpu.VMEM((384, 256), F32),
            pltpu.VMEM((16, QR, CH), BF16),
            pltpu.VMEM((EB, CH), F32),
            pltpu.VMEM((2, MB, CH), F32),
            dma((2,)),
            dma((6,)),
            dma((2,)),
            dma((7,)),
            dma((7,)),
            dma((2,)),
            dma((2,)),
            dma((6,)),
            dma((4,)),
            dma((2,)),
            dma((1,)),
            dma((23,)),
        ],
        compiler_params=pltpu.CompilerParams(
            collective_id=0, has_side_effects=True, vmem_limit_bytes=50 * 2**20
        ),
        name="cross_spectra",
    )(jnp.concatenate([source_blocks, band_bins]), raw_strain)
    return rows.reshape(SHARE, NB, 2, CH).transpose(0, 2, 1, 3).astype(BF16)


def solution(mesh):
    in_specs = (P("tm", "chan"), P(), P())
    out_specs = P("tm", None, None, "chan")
    return jax.shard_map(body, mesh=mesh, in_specs=in_specs, out_specs=out_specs, check_vma=False)
```

```python
import functools
import math

import jax
import jax.numpy as jnp
import numpy as np
from jax import lax
from jax.experimental import pallas as pl
from jax.experimental.pallas import tpu as pltpu
from jax.sharding import PartitionSpec as P

NW = 16
WIN = 500
NB = 20
VS = 640
TAPS = 64
DECIM = 4
CH = 128
ROWS = DECIM * NW * WIN
OUTS = NW * WIN
MB = 112
KB = 512
STEP = DECIM * MB
PAIRS = 36
HALO = 64
RAW_PAD = HALO + 2 * PAIRS * STEP
DEC_PAD = 2 * PAIRS * MB
EB = 256
EN_PAD = 8192
CHUNKS = (0, 6272, 11648, 17024, 22400, 27776, ROWS)
DR = 48
MAIN = 16
AR = 40
SR = 56
QR = 400
SHARE = 160
HR = QR // 2
FAR_FIRST = sorted(
    ((dy, dx) for dy in range(4) for dx in range(4) if dy or dx),
    key=lambda step: (-min(step[0], 4 - step[0]) - min(step[1], 4 - step[1]), step),
)
FR = 104
FORGET = math.exp(-1.0 / WIN)
F32 = jnp.float32
BF16 = jnp.bfloat16
MESH = pl.DeviceIdType.MESH


def lowpass_taps():
    offsets = np.arange(TAPS) - (TAPS - 1) / 2.0
    window = 0.54 - 0.46 * np.cos(2.0 * np.pi * np.arange(TAPS) / (TAPS - 1))
    angles = np.pi * 0.8 * offsets / DECIM
    values = np.sin(angles) / angles * window
    return values / values.sum()


def make_filter(filter_v):
    taps = lowpass_taps().astype(jnp.bfloat16).astype(np.float32)
    row = lax.broadcasted_iota(jnp.int32, (8, CH), 0)
    lane = lax.broadcasted_iota(jnp.int32, (8, CH), 1)
    lag = DECIM * row + DECIM - 1 + HALO - lane
    eight = jnp.zeros((8, CH), F32)
    for j in range(TAPS):
        eight = jnp.where(lag == j, float(taps[j]), eight)
    for b in range(MB // 16):
        rows = []
        for half in range(2):
            shift = 32 * (2 * b + half)
            turned = pltpu.roll(eight, shift % CH, axis=1) if shift % CH else eight
            columns = []
            for q in range(KB // CH):
                if q == shift // CH:
                    columns.append(jnp.where(lane >= shift % CH, turned, 0.0))
                elif q == shift // CH + 1:
                    columns.append(jnp.where(lane < shift % CH, turned, 0.0))
                else:
                    columns.append(jnp.zeros((8, CH), F32))
            rows.append(jnp.concatenate(columns, axis=1))
        filter_v[16 * b : 16 * b + 16, :] = jnp.concatenate(rows, axis=0).astype(BF16)


def make_tables(table_v, within_v, rising_v):
    place = lax.broadcasted_iota(jnp.int32, (EB, CH), 0).astype(F32)
    rising_v[...] = jnp.exp((place + 1.0) * (-1.0 / WIN))
    gap = lax.broadcasted_iota(jnp.int32, (EB, EB), 0) - lax.broadcasted_iota(jnp.int32, (EB, EB), 1)
    share = (1.0 - FORGET) * jnp.exp(jnp.maximum(gap, 0).astype(F32) * (-1.0 / WIN))
    within_v[...] = jnp.where(gap >= 0, share, 0.0).astype(BF16)
    row = lax.broadcasted_iota(jnp.int32, (DR, 512), 0)
    time = lax.broadcasted_iota(jnp.int32, (DR, 512), 1)
    late = row >= 2 * MAIN
    bin_id = jnp.where(late, MAIN + row % 4, row % MAIN)
    quarter = jnp.where(late, row // 4 % 2, row // MAIN % 2)
    angle = ((bin_id + 1) * time + (WIN // 4) * quarter).astype(F32)
    angle = angle - jnp.floor(angle * (1.0 / WIN)) * WIN
    angle = jnp.where(angle < 0.0, angle + WIN, jnp.where(angle >= WIN, angle - WIN, angle))
    angle = jnp.minimum(angle, WIN - angle)
    flip = angle > WIN / 4.0
    angle = jnp.where(flip, WIN / 2.0 - angle, angle)
    square = (angle * angle) * ((2.0 * math.pi / WIN) ** 2)
    cosine = jnp.full((DR, 512), 1.0, F32)
    for order in (14, 12, 10, 8, 6, 4, 2):
        cosine = 1.0 - square * cosine * (1.0 / (order * (order - 1)))
    cosine = jnp.where(flip, -cosine, cosine) * (1.0 / math.sqrt(WIN))
    cosine = jnp.where((time < WIN) & (row < 2 * NB), cosine, 0.0)
    for place in range(4):
        shifted = pltpu.roll(cosine, 4 * place, axis=1) if place else cosine
        table_v[place] = shifted.astype(BF16)


def kernel(
    small_hbm, raw_ref, out_ref,
    blocks_ref, table_v, filter_v, within_v, raw_v, dec_v, en_v, run_v, norm_v, white_v, total_v, totals_v,
    own_v, first_v, share_v, shares_v, rows_v, pieces_v, rising_v, weights_v, eye_v,
    small_sem, raw_sem, halo_sem, tot_ssem, tot_rsem, a_sem, b_sem, own_ssem, own_rsem, hand_sem, q_ssem, q_rsem,
):
    tm = lax.axis_index("tm")
    chan = lax.axis_index("chan")
    zl, core = tm // 2, tm % 2
    zh, pid = chan // 16, chan % 16
    y, x = pid // 4, pid % 4
    line = zh * 8 + tm
    totals_v[...] = jnp.zeros(totals_v.shape, F32)

    def repeat(count, step):
        lax.fori_loop(0, count, lambda n, carry: (step(n), carry)[1], 0)

    def unrolled(count, step):
        for n in range(count):
            step(n)

    def plane_device(other):
        return (tm, zh * 16 + other)

    def line_device(other):
        return (other % 8, (other // 8) * 16 + pid)

    def chunk(c):
        first, last = CHUNKS[c], CHUNKS[c + 1]
        return pltpu.make_async_copy(
            raw_ref.at[pl.ds(first, last - first)],
            raw_v.at[pl.ds(HALO + first, last - first)],
            raw_sem.at[c],
        )

    small = [
        pltpu.make_async_copy(source, target, small_sem.at[n])
        for n, (source, target) in enumerate(
            ((small_hbm, blocks_ref),)
        )
    ]
    for c in range(6):
        chunk(c).start()
    small[0].start()

    barrier = pltpu.get_barrier_semaphore()

    def greet(n):
        pl.semaphore_signal(
            barrier, inc=1, device_id=line_device((line + n + 1) % 16), device_id_type=MESH
        )
        pl.semaphore_signal(
            barrier, inc=1, device_id=plane_device((pid + n + 1) % 16), device_id_type=MESH
        )

    repeat(15, greet)

    raw_v[HALO + ROWS : RAW_PAD, :] = jnp.zeros((RAW_PAD - HALO - ROWS, CH), BF16)
    en_v[DEC_PAD:EN_PAD, :] = jnp.zeros((EN_PAD - DEC_PAD, CH), BF16)
    dec_v[DEC_PAD:EN_PAD, :] = jnp.zeros((EN_PAD - DEC_PAD, CH), F32)

    @pl.when(tm == 0)
    def _():
        raw_v[0:HALO, :] = jnp.zeros((HALO, CH), BF16)

    def halo_to(other):
        return pltpu.make_async_remote_copy(
            src_ref=raw_ref.at[pl.ds(ROWS - HALO, HALO)],
            dst_ref=raw_v.at[pl.ds(0, HALO)],
            send_sem=halo_sem.at[0],
            recv_sem=halo_sem.at[1],
            device_id=(other, chan),
            device_id_type=MESH,
        )

    tail = OUTS - (2 * PAIRS - 1) * MB
    back = lax.broadcasted_iota(jnp.int32, (MB, CH), 0).astype(F32) - (MB - 1.0)
    weights_v[0] = (1.0 - FORGET) * jnp.exp(back * (1.0 / WIN))
    back = back + float(MB - tail)
    weights_v[1] = jnp.where(
        back <= 0.0, (1.0 - FORGET) * jnp.exp(jnp.minimum(back, 0.0) * (1.0 / WIN)), 0.0
    )
    make_filter(filter_v)

    block_fade = FORGET**MB
    tail_fade = FORGET**tail

    def decimate(n, total):
        pair = (n + 1) % PAIRS
        is_tail, is_first = pair == PAIRS - 1, pair == 0
        start = pl.multiple_of(pair * (2 * STEP), 128)
        left = raw_v[pl.ds(start, KB), :]
        right = raw_v[pl.ds(start + STEP, KB), :]
        both = jnp.dot(
            filter_v[...], jnp.concatenate([left, right], axis=1), preferred_element_type=F32
        )
        row = pl.multiple_of(pair * (2 * MB), 32)
        sums = []
        for half in range(2):
            values = both[:, half * CH : (half + 1) * CH]
            dec_v[pl.ds(row + half * MB, MB), :] = values
            energy = values * values
            en_v[pl.ds(row + half * MB, MB), :] = energy.astype(BF16)
            weights = weights_v[0] if half == 0 else weights_v[pair // (PAIRS - 1)]
            sums.append(jnp.sum((weights * energy).reshape(MB // 8, 8, CH), axis=0))
        fade = jnp.where(is_tail, tail_fade, block_fade).astype(F32)
        decay = jnp.where(is_first, 1.0, block_fade * fade).astype(F32)
        gain = jnp.where(is_first, FORGET ** (OUTS - 2 * MB), 1.0).astype(F32)
        return total * decay + (sums[0] * fade + sums[1]) * gain

    def two_pairs(n, total):
        return decimate(n + 1, decimate(n, total))

    def stretch(c, total):
        for n in range(6):

            @pl.when(c == n)
            def _():
                chunk(n).wait()

        @pl.when(c == 4)
        def _():
            pl.semaphore_wait(barrier, 30)

            @pl.when(tm < 7)
            def _():
                halo_to(tm + 1).start()

        @pl.when((c == 5) & (tm > 0))
        def _():
            halo_to(tm - 1).wait_recv()

        return lax.fori_loop(0, 3, lambda n, t: two_pairs(6 * c + 2 * n, t), total)

    total = lax.fori_loop(0, 6, stretch, jnp.zeros((8, CH), F32))
    total_v[...] = jnp.broadcast_to(jnp.sum(total, axis=0, keepdims=True), (8, CH))

    def total_to(other, group, slot):
        return pltpu.make_async_remote_copy(
            src_ref=total_v,
            dst_ref=totals_v.at[group],
            send_sem=tot_ssem.at[slot],
            recv_sem=tot_rsem.at[group],
            device_id=(other, chan),
            device_id_type=MESH,
        )

    def total_sent(n):
        return total_to(tm + 1 + n, tm, n)

    lax.fori_loop(0, 7 - tm, lambda n, carry: (total_sent(n).start(), carry)[1], 0)
    make_tables(table_v, within_v, rising_v)

    def arrived(ref, sem):
        pltpu.make_async_remote_copy(
            src_ref=ref, dst_ref=ref, send_sem=sem, recv_sem=sem,
            device_id=plane_device((pid + 1) % 16), device_id_type=MESH,
        ).wait_recv()

    def departed(ref, sem):
        pltpu.make_async_remote_copy(
            src_ref=ref, dst_ref=ref, send_sem=sem, recv_sem=sem,
            device_id=plane_device((pid + 1) % 16), device_id_type=MESH,
        ).wait_send()

    def local_run(n):
        row = pl.multiple_of(n * (2 * EB), 2 * EB)
        rhs = jnp.concatenate([en_v[pl.ds(row, EB), :], en_v[pl.ds(row + EB, EB), :]], axis=1)
        both = jnp.dot(within_v[...], rhs, preferred_element_type=F32)
        run_v[pl.ds(row, EB), :] = both[:, :CH]
        run_v[pl.ds(row + EB, EB), :] = both[:, CH:]

    repeat(EN_PAD // (4 * EB), lambda n: (local_run(2 * n), local_run(2 * n + 1)))

    def total_taken(group, carry):
        total_to((tm + 1) % 8, group, 0).wait_recv()
        return carry

    lax.fori_loop(0, tm, total_taken, 0)

    state = jnp.zeros((8, CH), F32)
    for group in range(7):
        state = jnp.where(group < tm, state * math.exp(-NW) + totals_v[group], state)

    def normalize(block, state):
        row = pl.multiple_of(block * EB, EB)
        running = run_v[pl.ds(row, EB), :] + rising_v[...] * state[0:1, :]
        values = dec_v[pl.ds(row, EB), :] * lax.rsqrt(jnp.maximum(running, 0.01))
        norm_v[pl.ds(row, EB), :] = values.astype(BF16)
        return jnp.broadcast_to(running[EB - 1 : EB, :], (8, CH))

    lax.fori_loop(
        0, EN_PAD // (2 * EB), lambda n, s: normalize(2 * n + 1, normalize(2 * n, s)), state
    )

    small[0].wait()
    low, high = blocks_ref[2], blocks_ref[3]
    row_id = lax.broadcasted_iota(jnp.int32, (2 * NB, CH), 0)
    bin_id = jnp.where(row_id < 2 * MAIN, row_id % MAIN, MAIN + row_id % 4)
    keep = jnp.where((bin_id >= low) & (bin_id < high), 1.0, 0.0).astype(F32)

    def spectra_of(n):
        first = n + n // 4 * 4
        start = first * WIN // 16 * 16
        rhs = jnp.concatenate(
            [norm_v[pl.ds(start, 512), :], norm_v[pl.ds(start + 4 * WIN, 512), :]], axis=1
        )
        both = jnp.dot(table_v[first * WIN % 16 // 4], rhs, preferred_element_type=F32)
        for half in range(2):
            w = first + 4 * half
            spectra = both[: 2 * NB, half * CH : (half + 1) * CH]
            power = jnp.sum(spectra * spectra, axis=0, keepdims=True) / NB
            white = spectra * keep * lax.rsqrt(jnp.maximum(power, 0.1))
            for p in range(2):
                white_v[pl.ds(p * NW + w, MAIN, stride=AR), :] = white[p * MAIN : (p + 1) * MAIN]
                white_v[pl.ds(w // 4 * (4 * AR) + 32 + p * 4 + w % 4, 4, stride=AR), :] = white[
                    32 + 4 * p : 36 + 4 * p
                ]

    unrolled(8, spectra_of)
    own_v[tm] = white_v[...].reshape(MAIN, AR, CH).astype(BF16)

    def plane_copy(other):
        return pltpu.make_async_remote_copy(
            src_ref=own_v.at[tm, other],
            dst_ref=first_v.at[pid],
            send_sem=a_sem.at[0],
            recv_sem=a_sem.at[1],
            device_id=plane_device(other),
            device_id_type=MESH,
        )

    for dy, dx in FAR_FIRST:
        plane_copy((y + dy) % 4 * 4 + (x + dx) % 4).start()

    def own_copy(group, other, slot, arrival):
        return pltpu.make_async_remote_copy(
            src_ref=own_v.at[group],
            dst_ref=own_v.at[group],
            send_sem=own_ssem.at[slot],
            recv_sem=arrival,
            device_id=(other, chan),
            device_id_type=MESH,
        )

    partner = zl * 2 + 1 - core

    def hand_over(group):
        return pltpu.make_async_remote_copy(
            src_ref=own_v.at[group],
            dst_ref=own_v.at[group],
            send_sem=hand_sem.at[0],
            recv_sem=hand_sem.at[1],
            device_id=(partner, chan),
            device_id_type=MESH,
        )

    sends = []

    def send_along(condition, group, other, slot):
        sends.append((condition, group, other, slot))

        @pl.when(condition)
        def _():
            own_copy(group, other, slot, own_rsem.at[group // 2]).start()

    send_along(zl < 3, tm, tm + 2, 0)
    send_along(zl > 0, tm, tm - 2, 1)
    hand_over(tm).start()

    def relay_own(step):
        below, above = tm - 2 * step, tm + 2 * step

        @pl.when(zl - step >= 0)
        def _():
            own_copy(below, partner, 0, own_rsem.at[below // 2]).wait_recv()

        @pl.when(zl + step <= 3)
        def _():
            own_copy(above, partner, 0, own_rsem.at[above // 2]).wait_recv()

        if step < 3:
            send_along((zl - step >= 0) & (zl < 3), below, tm + 2, 2 * step)
            send_along((zl + step <= 3) & (zl > 0), above, tm - 2, 2 * step + 1)

        @pl.when(zl - step >= 0)
        def _():
            hand_over(below).start()

        @pl.when(zl + step <= 3)
        def _():
            hand_over(above).start()

    eye = (
        lax.broadcasted_iota(jnp.int32, (SHARE, 256), 0)
        == lax.broadcasted_iota(jnp.int32, (SHARE, 256), 1)
    )
    eye_v[...] = jnp.where(eye, 1.0, 0.0).astype(BF16)
    first_v[pid] = own_v[tm, pid]
    arrived(first_v.at[pl.ds(0, 15)], a_sem.at[1])

    lane8 = lax.broadcasted_iota(jnp.int32, (8, CH), 1)
    lane40 = lax.broadcasted_iota(jnp.int32, (AR, CH), 1)

    def turn_left(rows, lanes):
        return pltpu.roll(rows, CH - lanes, axis=1) if lanes else rows

    picked = []
    for b in range(2):
        for i in range(5):
            block = blocks_ref[b] + i
            here = jnp.where(block // 16 == zh, 1.0, 0.0).astype(F32)
            picked.append(first_v[block % 16].astype(F32) * here)
    for share in range(8):
        jj = share % 4
        a, c = picked[share // 4 * 5 + jj], picked[share // 4 * 5 + jj + 1]
        turned = turn_left(c, 32 * jj)
        head = jnp.where(lane40 < CH - 32 * jj, turn_left(a, 32 * jj), turned)
        rest = jnp.where(lane8 < 32, turned[0:8], 0.0)
        for q in range(1, 4):
            part = pltpu.roll(turned[8 * q : 8 * q + 8], 32 * q, axis=1)
            rest = jnp.where((lane8 >= 32 * q) & (lane8 < 32 * q + 32), part, rest)
        last_rest = jnp.where(lane8 < 32, turned[32:40], 0.0)
        share_v[share] = jnp.concatenate([head, rest, last_rest], axis=0).astype(BF16)

    def line_copy(other):
        return pltpu.make_async_remote_copy(
            src_ref=share_v.at[other % 8],
            dst_ref=shares_v.at[line],
            send_sem=b_sem.at[0],
            recv_sem=b_sem.at[1],
            device_id=line_device(other),
            device_id_type=MESH,
        )

    for dz in (4, 3, 5, 2, 6, 1, 7):
        for dc in range(2):
            line_copy((line // 2 + dz) % 8 * 2 + (core + dc) % 2).start()
    line_copy(line + 1 - 2 * core).start()
    shares_v[line] = share_v[tm]
    relay_own(1)
    arrived(shares_v.at[pl.ds(0, 15)], b_sem.at[1])

    def unpack(g):
        both = shares_v[g].astype(F32) + shares_v[8 + g].astype(F32)
        rests = [both[40:48]]
        for q in range(1, 4):
            rests.append(pltpu.roll(both[40:48], CH - 32 * q, axis=1))
        rests.append(both[48:56])
        rows = jnp.concatenate([both[0:40], jnp.concatenate(rests, axis=0)], axis=1)
        rows_v[pl.ds(pl.multiple_of(g * 32, 32), 32), :] = rows[0:32]
        rows_v[pl.ds(pl.multiple_of(256 + g * 8, 8), 8), :] = rows[32:40]
        rows_v[pl.ds(pl.multiple_of(320 + g * 8, 8), 8), :] = rows[32:40]

    unrolled(8, unpack)
    turned = lax.dot_general(
        eye_v[...], rows_v[...].astype(BF16), (((1,), (1,)), ((), ())), preferred_element_type=F32
    )
    half_lane = lax.broadcasted_iota(jnp.int32, (80, CH), 1) < 64
    packed_tail = jnp.where(half_lane, turned[0:80, 2 * CH :], turned[80:160, 2 * CH :])
    pieces_v[pid] = jnp.concatenate(
        [turned[:, :CH], turned[:, CH : 2 * CH], packed_tail], axis=0
    ).astype(BF16)

    def at(h, f, s):
        dx, dy = f * (1 - h) + s * h, f * h + s * (1 - h)
        return ((y + dy) % 4) * 4 + (x + dx) % 4

    def piece_copy(h, f, s, along, across, first, count, event):
        rows = pl.ds(pl.multiple_of(h * HR + first, 8), count)
        return pltpu.make_async_remote_copy(
            src_ref=pieces_v.at[at(h, f, s), rows],
            dst_ref=pieces_v.at[at(h, f, s), rows],
            send_sem=q_ssem.at[0],
            recv_sem=q_rsem.at[event],
            device_id=plane_device(at(h, along, across)),
            device_id_type=MESH,
        )

    def wait_half(h, f, s, event):
        piece_copy(h, f, s, 1, 0, 0, HR, event).wait_recv()

    def send_across(h, f):
        for t in range(2):
            piece_copy(h, f, 0, 0, 1 + 2 * t, 0, HR, h * 11 + 3 + 2 * f + t).start()

    def forward(h, f, s, along, t, event):
        first, count = ((0, FR), (FR, HR - FR))[t]
        step = 1 + 2 * t
        piece_copy(
            h, f, s, step if along else 0, 0 if along else step, first, count, event
        ).start()

    def along_rows(t, late):
        return ((0, FR), (FR, HR - FR))[t if late == 0 else 1 - t]

    def own_half(h):
        for late in range(2):
            for t in range(2):
                event = h * 11 + t if late == 0 else 23 + 2 * h + t
                first, count = along_rows(t, late)
                piece_copy(h, 0, 0, 1 + 2 * t, 0, first, count, event).start()

    def near_along(h):
        for t in range(2):
            piece_copy(h, 3 - 2 * t, 0, 1, 0, *along_rows(t, 0), h * 11 + t).wait_recv()
            forward(h, 3 - 2 * t, 0, True, t, h * 11 + 2)

    def near_spread(h):
        for t in range(2):
            piece_copy(h, 3 - 2 * t, 0, 1, 0, *along_rows(t, 1), 23 + 2 * h + t).wait_recv()
            send_across(h, 3 - 2 * t)

    def near_across(h, f):
        for t in range(2):
            wait_half(h, f, 3 - 2 * t, h * 11 + 3 + 2 * f + t)
            forward(h, f, 3 - 2 * t, False, t, 22)

    def far_along(h):
        wait_half(h, 2, 0, h * 11 + 2)
        send_across(h, 2)

    repeat(2, own_half)
    repeat(2, lambda h: send_across(h, 0))
    relay_own(2)
    repeat(2, near_along)
    repeat(2, near_spread)
    repeat(2, lambda h: near_across(h, 0))
    repeat(2, far_along)
    relay_own(3)

    scale = 1.0 / math.sqrt(8 * NW)

    def put(k, lhs, rhs):
        both = jnp.dot(lhs, rhs, preferred_element_type=F32) * scale
        out_ref[pl.ds(2 * k, SHARE, stride=2 * NB), :] = both[:, :CH]
        out_ref[pl.ds(2 * k + 1, SHARE, stride=2 * NB), :] = both[:, CH:]

    def main_bin(k):
        lhs = jnp.concatenate([pieces_v[k, 0:SHARE], pieces_v[k, SHARE : 2 * SHARE]], axis=1)
        re, im = [], []
        for g in range(8):
            rows = own_v[g, k, 0:32]
            re.append(rows)
            im.append(rows[16:32])
            im.append(-rows[0:16])
        rhs = jnp.concatenate([jnp.concatenate(re, axis=0), jnp.concatenate(im, axis=0)], axis=1)
        put(k, lhs, rhs)

    sign = jnp.where(lax.broadcasted_iota(jnp.int32, (8, CH), 0) < 4, 1.0, -1.0).astype(F32)

    def tail_bin(kk):
        columns = []
        for pair in range(2):
            even = pieces_v[pair * 8 + kk, 2 * SHARE : QR].astype(F32)
            odd = pieces_v[pair * 8 + 4 + kk, 2 * SHARE : QR].astype(F32)
            upper = jnp.where(half_lane, even, pltpu.roll(odd, 64, axis=1))
            lower = jnp.where(half_lane, pltpu.roll(even, 64, axis=1), odd)
            columns.append(jnp.concatenate([upper, lower], axis=0))
        lhs = jnp.concatenate(columns, axis=1).astype(BF16)
        re, im = [], []
        for wh in range(4):
            for g in range(8):
                rows = own_v[g, wh * 4 + kk, 32:40].astype(F32)
                re.append(rows)
                im.append(pltpu.roll(rows, 4, axis=0) * sign)
        rhs = jnp.concatenate([jnp.concatenate(re, axis=0), jnp.concatenate(im, axis=0)], axis=1)
        put(MAIN + kk, lhs, rhs.astype(BF16))

    repeat(2, lambda h: near_across(h, 1))
    arrived(own_v.at[pl.ds(0, 4)], hand_sem.at[1])
    main_bin(pid)
    main_bin(at(0, 1, 0))
    repeat(2, lambda h: near_across(h, 3))
    main_bin(at(0, 3, 0))
    main_bin(at(0, 0, 1))
    repeat(2, lambda h: near_across(h, 2))
    main_bin(at(0, 0, 3))
    for f in (1, 3):
        for s in (1, 3):
            main_bin(at(0, f, s))
    arrived(pieces_v.at[pl.ds(0, 4)], q_rsem.at[22])
    for f, s in ((2, 0), (2, 1), (2, 2), (2, 3), (0, 2), (1, 2), (3, 2)):
        main_bin(at(0, f, s))
    unrolled(NB - MAIN, tail_bin)

    @pl.when(tm < 7)
    def _():
        halo_to(tm + 1).wait_send()

    lax.fori_loop(0, 7 - tm, lambda n, carry: (total_sent(n).wait_send(), carry)[1], 0)
    departed(first_v.at[pl.ds(0, 15)], a_sem.at[0])
    departed(shares_v.at[pl.ds(0, 15)], b_sem.at[0])
    departed(own_v.at[pl.ds(0, 4)], hand_sem.at[0])
    departed(pieces_v.at[pl.ds(0, 15)], q_ssem.at[0])
    for condition, group, other, slot in sends:

        @pl.when(condition)
        def _():
            own_copy(group, other, slot, own_rsem.at[0]).wait_send()


def body(raw_strain, source_blocks, band_bins):
    hbm = pl.BlockSpec(memory_space=pltpu.HBM)
    vmem = pl.BlockSpec(memory_space=pltpu.VMEM)
    dma = pltpu.SemaphoreType.DMA
    rows = pl.pallas_call(
        kernel,
        out_shape=jax.ShapeDtypeStruct((SHARE * NB * 2, CH), F32),
        in_specs=[hbm] * 2,
        out_specs=vmem,
        scratch_shapes=[
            pltpu.SMEM((4,), jnp.int32),
            pltpu.VMEM((4, DR, 512), BF16),
            pltpu.VMEM((MB, KB), BF16),
            pltpu.VMEM((EB, EB), BF16),
            pltpu.VMEM((RAW_PAD, CH), BF16),
            pltpu.VMEM((EN_PAD, CH), F32),
            pltpu.VMEM((EN_PAD, CH), BF16),
            pltpu.VMEM((EN_PAD, CH), F32),
            pltpu.VMEM((EN_PAD, CH), BF16),
            pltpu.VMEM((MAIN * AR, CH), F32),
            pltpu.VMEM((8, CH), F32),
            pltpu.VMEM((8, 8, CH), F32),
            pltpu.VMEM((8, MAIN, AR, CH), BF16),
            pltpu.VMEM((16, AR, CH), BF16),
            pltpu.VMEM((8, SR, CH), BF16),
            pltpu.VMEM((16, SR, CH), BF16),
            pltpu.VMEM((384, 256), F32),
            pltpu.VMEM((16, QR, CH), BF16),
            pltpu.VMEM((EB, CH), F32),
            pltpu.VMEM((2, MB, CH), F32),
            pltpu.VMEM((SHARE, 256), BF16),
            dma((2,)),
            dma((6,)),
            dma((2,)),
            dma((7,)),
            dma((7,)),
            dma((2,)),
            dma((2,)),
            dma((6,)),
            dma((4,)),
            dma((2,)),
            dma((1,)),
            dma((27,)),
        ],
        compiler_params=pltpu.CompilerParams(
            collective_id=0, has_side_effects=True, vmem_limit_bytes=50 * 2**20
        ),
        name="cross_spectra",
    )(jnp.concatenate([source_blocks, band_bins]), raw_strain)
    return rows.reshape(SHARE, NB, 2, CH).transpose(0, 2, 1, 3).astype(BF16)


def solution(mesh):
    in_specs = (P("tm", "chan"), P(), P())
    out_specs = P("tm", None, None, "chan")
    return jax.shard_map(body, mesh=mesh, in_specs=in_specs, out_specs=out_specs, check_vma=False)
```

```python
import functools
import math

import jax
import jax.numpy as jnp
import numpy as np
from jax import lax
from jax.experimental import pallas as pl
from jax.experimental.pallas import tpu as pltpu
from jax.sharding import PartitionSpec as P

NW = 16
WIN = 500
NB = 20
VS = 640
TAPS = 64
DECIM = 4
CH = 128
ROWS = DECIM * NW * WIN
OUTS = NW * WIN
MB = 112
KB = 512
STEP = DECIM * MB
PAIRS = 36
HALO = 64
RAW_PAD = HALO + 2 * PAIRS * STEP
DEC_PAD = 2 * PAIRS * MB
EB = 256
EN_PAD = 8192
CHUNKS = (0, 6272, 11648, 17024, 22400, 27776, ROWS)
DR = 48
MAIN = 16
AR = 40
SR = 56
QR = 400
SHARE = 160
HR = QR // 2
FAR_FIRST = sorted(
    ((dy, dx) for dy in range(4) for dx in range(4) if dy or dx),
    key=lambda step: (-min(step[0], 4 - step[0]) - min(step[1], 4 - step[1]), step),
)
FR = 104
FORGET = math.exp(-1.0 / WIN)
F32 = jnp.float32
BF16 = jnp.bfloat16
MESH = pl.DeviceIdType.MESH


def lowpass_taps():
    offsets = np.arange(TAPS) - (TAPS - 1) / 2.0
    window = 0.54 - 0.46 * np.cos(2.0 * np.pi * np.arange(TAPS) / (TAPS - 1))
    angles = np.pi * 0.8 * offsets / DECIM
    values = np.sin(angles) / angles * window
    return values / values.sum()


def make_filter(filter_v):
    taps = lowpass_taps().astype(jnp.bfloat16).astype(np.float32)
    row = lax.broadcasted_iota(jnp.int32, (8, CH), 0)
    lane = lax.broadcasted_iota(jnp.int32, (8, CH), 1)
    lag = DECIM * row + DECIM - 1 + HALO - lane
    eight = jnp.zeros((8, CH), F32)
    for j in range(TAPS):
        eight = jnp.where(lag == j, float(taps[j]), eight)
    for b in range(MB // 16):
        rows = []
        for half in range(2):
            shift = 32 * (2 * b + half)
            turned = pltpu.roll(eight, shift % CH, axis=1) if shift % CH else eight
            columns = []
            for q in range(KB // CH):
                if q == shift // CH:
                    columns.append(jnp.where(lane >= shift % CH, turned, 0.0))
                elif q == shift // CH + 1:
                    columns.append(jnp.where(lane < shift % CH, turned, 0.0))
                else:
                    columns.append(jnp.zeros((8, CH), F32))
            rows.append(jnp.concatenate(columns, axis=1))
        filter_v[16 * b : 16 * b + 16, :] = jnp.concatenate(rows, axis=0).astype(BF16)


def make_tables(table_v, within_v, rising_v):
    place = lax.broadcasted_iota(jnp.int32, (EB, CH), 0).astype(F32)
    rising_v[...] = jnp.exp((place + 1.0) * (-1.0 / WIN))
    gap = lax.broadcasted_iota(jnp.int32, (EB, EB), 0) - lax.broadcasted_iota(jnp.int32, (EB, EB), 1)
    share = (1.0 - FORGET) * jnp.exp(jnp.maximum(gap, 0).astype(F32) * (-1.0 / WIN))
    within_v[...] = jnp.where(gap >= 0, share, 0.0).astype(BF16)
    row = lax.broadcasted_iota(jnp.int32, (DR, 512), 0)
    time = lax.broadcasted_iota(jnp.int32, (DR, 512), 1)
    late = row >= 2 * MAIN
    bin_id = jnp.where(late, MAIN + row % 4, row % MAIN)
    quarter = jnp.where(late, row // 4 % 2, row // MAIN % 2)
    angle = ((bin_id + 1) * time + (WIN // 4) * quarter).astype(F32)
    angle = angle - jnp.floor(angle * (1.0 / WIN)) * WIN
    angle = jnp.where(angle < 0.0, angle + WIN, jnp.where(angle >= WIN, angle - WIN, angle))
    angle = jnp.minimum(angle, WIN - angle)
    flip = angle > WIN / 4.0
    angle = jnp.where(flip, WIN / 2.0 - angle, angle)
    square = (angle * angle) * ((2.0 * math.pi / WIN) ** 2)
    cosine = jnp.full((DR, 512), 1.0, F32)
    for order in (14, 12, 10, 8, 6, 4, 2):
        cosine = 1.0 - square * cosine * (1.0 / (order * (order - 1)))
    cosine = jnp.where(flip, -cosine, cosine) * (1.0 / math.sqrt(WIN))
    cosine = jnp.where((time < WIN) & (row < 2 * NB), cosine, 0.0)
    for place in range(4):
        shifted = pltpu.roll(cosine, 4 * place, axis=1) if place else cosine
        table_v[place] = shifted.astype(BF16)


def kernel(
    small_hbm, raw_ref, out_ref,
    blocks_ref, table_v, filter_v, within_v, raw_v, dec_v, en_v, run_v, norm_v, white_v, total_v, totals_v,
    own_v, first_v, share_v, shares_v, rows_v, pieces_v, rising_v, weights_v, eye_v,
    small_sem, raw_sem, halo_sem, tot_ssem, tot_rsem, a_sem, b_sem, own_ssem, own_rsem, hand_sem, q_ssem, q_rsem,
):
    tm = lax.axis_index("tm")
    chan = lax.axis_index("chan")
    zl, core = tm // 2, tm % 2
    zh, pid = chan // 16, chan % 16
    y, x = pid // 4, pid % 4
    line = zh * 8 + tm
    totals_v[...] = jnp.zeros(totals_v.shape, F32)

    def repeat(count, step):
        lax.fori_loop(0, count, lambda n, carry: (step(n), carry)[1], 0)

    def unrolled(count, step):
        for n in range(count):
            step(n)

    def plane_device(other):
        return (tm, zh * 16 + other)

    def line_device(other):
        return (other % 8, (other // 8) * 16 + pid)

    def chunk(c):
        first, last = CHUNKS[c], CHUNKS[c + 1]
        return pltpu.make_async_copy(
            raw_ref.at[pl.ds(first, last - first)],
            raw_v.at[pl.ds(HALO + first, last - first)],
            raw_sem.at[c],
        )

    small = [
        pltpu.make_async_copy(source, target, small_sem.at[n])
        for n, (source, target) in enumerate(
            ((small_hbm, blocks_ref),)
        )
    ]
    for c in range(6):
        chunk(c).start()
    small[0].start()

    barrier = pltpu.get_barrier_semaphore()

    def greet(n):
        pl.semaphore_signal(
            barrier, inc=1, device_id=line_device((line + n + 1) % 16), device_id_type=MESH
        )
        pl.semaphore_signal(
            barrier, inc=1, device_id=plane_device((pid + n + 1) % 16), device_id_type=MESH
        )

    repeat(15, greet)

    raw_v[HALO + ROWS : RAW_PAD, :] = jnp.zeros((RAW_PAD - HALO - ROWS, CH), BF16)
    en_v[DEC_PAD:EN_PAD, :] = jnp.zeros((EN_PAD - DEC_PAD, CH), BF16)
    dec_v[DEC_PAD:EN_PAD, :] = jnp.zeros((EN_PAD - DEC_PAD, CH), F32)

    @pl.when(tm == 0)
    def _():
        raw_v[0:HALO, :] = jnp.zeros((HALO, CH), BF16)

    def halo_to(other):
        return pltpu.make_async_remote_copy(
            src_ref=raw_ref.at[pl.ds(ROWS - HALO, HALO)],
            dst_ref=raw_v.at[pl.ds(0, HALO)],
            send_sem=halo_sem.at[0],
            recv_sem=halo_sem.at[1],
            device_id=(other, chan),
            device_id_type=MESH,
        )

    tail = OUTS - (2 * PAIRS - 1) * MB
    back = lax.broadcasted_iota(jnp.int32, (MB, CH), 0).astype(F32) - (MB - 1.0)
    weights_v[0] = (1.0 - FORGET) * jnp.exp(back * (1.0 / WIN))
    back = back + float(MB - tail)
    weights_v[1] = jnp.where(
        back <= 0.0, (1.0 - FORGET) * jnp.exp(jnp.minimum(back, 0.0) * (1.0 / WIN)), 0.0
    )
    make_filter(filter_v)

    block_fade = FORGET**MB
    tail_fade = FORGET**tail

    def decimate(n, total):
        pair = (n + 1) % PAIRS
        is_tail, is_first = pair == PAIRS - 1, pair == 0
        start = pl.multiple_of(pair * (2 * STEP), 128)
        left = raw_v[pl.ds(start, KB), :]
        right = raw_v[pl.ds(start + STEP, KB), :]
        both = jnp.dot(
            filter_v[...], jnp.concatenate([left, right], axis=1), preferred_element_type=F32
        )
        row = pl.multiple_of(pair * (2 * MB), 32)
        sums = []
        for half in range(2):
            values = both[:, half * CH : (half + 1) * CH]
            dec_v[pl.ds(row + half * MB, MB), :] = values
            energy = values * values
            en_v[pl.ds(row + half * MB, MB), :] = energy.astype(BF16)
            weights = weights_v[0] if half == 0 else weights_v[pair // (PAIRS - 1)]
            sums.append(jnp.sum((weights * energy).reshape(MB // 8, 8, CH), axis=0))
        fade = jnp.where(is_tail, tail_fade, block_fade).astype(F32)
        decay = jnp.where(is_first, 1.0, block_fade * fade).astype(F32)
        gain = jnp.where(is_first, FORGET ** (OUTS - 2 * MB), 1.0).astype(F32)
        return total * decay + (sums[0] * fade + sums[1]) * gain

    def two_pairs(n, total):
        return decimate(n + 1, decimate(n, total))

    def stretch(c, total):
        for n in range(6):

            @pl.when(c == n)
            def _():
                chunk(n).wait()

        @pl.when(c == 4)
        def _():
            pl.semaphore_wait(barrier, 30)

            @pl.when(tm < 7)
            def _():
                halo_to(tm + 1).start()

        @pl.when((c == 5) & (tm > 0))
        def _():
            halo_to(tm - 1).wait_recv()

        return lax.fori_loop(0, 3, lambda n, t: two_pairs(6 * c + 2 * n, t), total)

    total = lax.fori_loop(0, 6, stretch, jnp.zeros((8, CH), F32))
    total_v[...] = jnp.broadcast_to(jnp.sum(total, axis=0, keepdims=True), (8, CH))

    def total_to(other, group, slot):
        return pltpu.make_async_remote_copy(
            src_ref=total_v,
            dst_ref=totals_v.at[group],
            send_sem=tot_ssem.at[slot],
            recv_sem=tot_rsem.at[group],
            device_id=(other, chan),
            device_id_type=MESH,
        )

    def total_sent(n):
        return total_to(tm + 1 + n, tm, n)

    lax.fori_loop(0, 7 - tm, lambda n, carry: (total_sent(n).start(), carry)[1], 0)
    make_tables(table_v, within_v, rising_v)

    def arrived(ref, sem):
        pltpu.make_async_remote_copy(
            src_ref=ref, dst_ref=ref, send_sem=sem, recv_sem=sem,
            device_id=plane_device((pid + 1) % 16), device_id_type=MESH,
        ).wait_recv()

    def departed(ref, sem):
        pltpu.make_async_remote_copy(
            src_ref=ref, dst_ref=ref, send_sem=sem, recv_sem=sem,
            device_id=plane_device((pid + 1) % 16), device_id_type=MESH,
        ).wait_send()

    def local_run(n):
        row = pl.multiple_of(n * (2 * EB), 2 * EB)
        rhs = jnp.concatenate([en_v[pl.ds(row, EB), :], en_v[pl.ds(row + EB, EB), :]], axis=1)
        both = jnp.dot(within_v[...], rhs, preferred_element_type=F32)
        run_v[pl.ds(row, EB), :] = both[:, :CH]
        run_v[pl.ds(row + EB, EB), :] = both[:, CH:]

    repeat(EN_PAD // (4 * EB), lambda n: (local_run(2 * n), local_run(2 * n + 1)))

    def total_taken(group, carry):
        total_to((tm + 1) % 8, group, 0).wait_recv()
        return carry

    lax.fori_loop(0, tm, total_taken, 0)

    state = jnp.zeros((8, CH), F32)
    for group in range(7):
        state = jnp.where(group < tm, state * math.exp(-NW) + totals_v[group], state)

    def normalize(block, state):
        row = pl.multiple_of(block * EB, EB)
        running = run_v[pl.ds(row, EB), :] + rising_v[...] * state[0:1, :]
        values = dec_v[pl.ds(row, EB), :] * lax.rsqrt(jnp.maximum(running, 0.01))
        norm_v[pl.ds(row, EB), :] = values.astype(BF16)
        return jnp.broadcast_to(running[EB - 1 : EB, :], (8, CH))

    lax.fori_loop(
        0, EN_PAD // (2 * EB), lambda n, s: normalize(2 * n + 1, normalize(2 * n, s)), state
    )

    small[0].wait()
    low, high = blocks_ref[2], blocks_ref[3]
    row_id = lax.broadcasted_iota(jnp.int32, (2 * NB, CH), 0)
    bin_id = jnp.where(row_id < 2 * MAIN, row_id % MAIN, MAIN + row_id % 4)
    keep = jnp.where((bin_id >= low) & (bin_id < high), 1.0, 0.0).astype(F32)

    def spectra_of(n):
        first = n + n // 4 * 4
        start = first * WIN // 16 * 16
        rhs = jnp.concatenate(
            [norm_v[pl.ds(start, 512), :], norm_v[pl.ds(start + 4 * WIN, 512), :]], axis=1
        )
        both = jnp.dot(table_v[first * WIN % 16 // 4], rhs, preferred_element_type=F32)
        for half in range(2):
            w = first + 4 * half
            spectra = both[: 2 * NB, half * CH : (half + 1) * CH]
            power = jnp.sum(spectra * spectra, axis=0, keepdims=True) / NB
            white = spectra * keep * lax.rsqrt(jnp.maximum(power, 0.1))
            for p in range(2):
                white_v[pl.ds(p * NW + w, MAIN, stride=AR), :] = white[p * MAIN : (p + 1) * MAIN]
                white_v[pl.ds(w // 4 * (4 * AR) + 32 + p * 4 + w % 4, 4, stride=AR), :] = white[
                    32 + 4 * p : 36 + 4 * p
                ]

    unrolled(8, spectra_of)
    own_v[tm] = white_v[...].reshape(MAIN, AR, CH).astype(BF16)

    def plane_copy(other):
        return pltpu.make_async_remote_copy(
            src_ref=own_v.at[tm, other],
            dst_ref=first_v.at[pid],
            send_sem=a_sem.at[0],
            recv_sem=a_sem.at[1],
            device_id=plane_device(other),
            device_id_type=MESH,
        )

    for dy, dx in FAR_FIRST:
        plane_copy((y + dy) % 4 * 4 + (x + dx) % 4).start()

    def own_copy(group, other, slot, arrival):
        return pltpu.make_async_remote_copy(
            src_ref=own_v.at[group],
            dst_ref=own_v.at[group],
            send_sem=own_ssem.at[slot],
            recv_sem=arrival,
            device_id=(other, chan),
            device_id_type=MESH,
        )

    partner = zl * 2 + 1 - core

    def hand_over(group):
        return pltpu.make_async_remote_copy(
            src_ref=own_v.at[group],
            dst_ref=own_v.at[group],
            send_sem=hand_sem.at[0],
            recv_sem=hand_sem.at[1],
            device_id=(partner, chan),
            device_id_type=MESH,
        )

    sends = []

    def send_along(condition, group, other, slot):
        sends.append((condition, group, other, slot))

        @pl.when(condition)
        def _():
            own_copy(group, other, slot, own_rsem.at[group // 2]).start()

    send_along(zl < 3, tm, tm + 2, 0)
    send_along(zl > 0, tm, tm - 2, 1)
    hand_over(tm).start()

    def relay_own(step):
        below, above = tm - 2 * step, tm + 2 * step

        @pl.when(zl - step >= 0)
        def _():
            own_copy(below, partner, 0, own_rsem.at[below // 2]).wait_recv()

        @pl.when(zl + step <= 3)
        def _():
            own_copy(above, partner, 0, own_rsem.at[above // 2]).wait_recv()

        if step < 3:
            send_along((zl - step >= 0) & (zl < 3), below, tm + 2, 2 * step)
            send_along((zl + step <= 3) & (zl > 0), above, tm - 2, 2 * step + 1)

        @pl.when(zl - step >= 0)
        def _():
            hand_over(below).start()

        @pl.when(zl + step <= 3)
        def _():
            hand_over(above).start()

    eye = (
        lax.broadcasted_iota(jnp.int32, (SHARE, 256), 0)
        == lax.broadcasted_iota(jnp.int32, (SHARE, 256), 1)
    )
    eye_v[...] = jnp.where(eye, 1.0, 0.0).astype(BF16)
    first_v[pid] = own_v[tm, pid]
    arrived(first_v.at[pl.ds(0, 15)], a_sem.at[1])

    lane8 = lax.broadcasted_iota(jnp.int32, (8, CH), 1)
    lane40 = lax.broadcasted_iota(jnp.int32, (AR, CH), 1)

    def turn_left(rows, lanes):
        return pltpu.roll(rows, CH - lanes, axis=1) if lanes else rows

    picked = []
    for b in range(2):
        for i in range(5):
            block = blocks_ref[b] + i
            here = jnp.where(block // 16 == zh, 1.0, 0.0).astype(F32)
            picked.append(first_v[block % 16].astype(F32) * here)
    for share in range(8):
        jj = share % 4
        a, c = picked[share // 4 * 5 + jj], picked[share // 4 * 5 + jj + 1]
        turned = turn_left(c, 32 * jj)
        head = jnp.where(lane40 < CH - 32 * jj, turn_left(a, 32 * jj), turned)
        rest = jnp.where(lane8 < 32, turned[0:8], 0.0)
        for q in range(1, 4):
            part = pltpu.roll(turned[8 * q : 8 * q + 8], 32 * q, axis=1)
            rest = jnp.where((lane8 >= 32 * q) & (lane8 < 32 * q + 32), part, rest)
        last_rest = jnp.where(lane8 < 32, turned[32:40], 0.0)
        share_v[share] = jnp.concatenate([head, rest, last_rest], axis=0).astype(BF16)

    def line_copy(other):
        return pltpu.make_async_remote_copy(
            src_ref=share_v.at[other % 8],
            dst_ref=shares_v.at[line],
            send_sem=b_sem.at[0],
            recv_sem=b_sem.at[1],
            device_id=line_device(other),
            device_id_type=MESH,
        )

    for dz in (4, 3, 5, 2, 6, 1, 7):
        for dc in range(2):
            line_copy((line // 2 + dz) % 8 * 2 + (core + dc) % 2).start()
    line_copy(line + 1 - 2 * core).start()
    shares_v[line] = share_v[tm]
    relay_own(1)
    arrived(shares_v.at[pl.ds(0, 15)], b_sem.at[1])

    def unpack(g):
        both = shares_v[g].astype(F32) + shares_v[8 + g].astype(F32)
        rests = [both[40:48]]
        for q in range(1, 4):
            rests.append(pltpu.roll(both[40:48], CH - 32 * q, axis=1))
        rests.append(both[48:56])
        rows = jnp.concatenate([both[0:40], jnp.concatenate(rests, axis=0)], axis=1)
        rows_v[pl.ds(pl.multiple_of(g * 32, 32), 32), :] = rows[0:32]
        rows_v[pl.ds(pl.multiple_of(256 + g * 8, 8), 8), :] = rows[32:40]
        rows_v[pl.ds(pl.multiple_of(320 + g * 8, 8), 8), :] = rows[32:40]

    unrolled(8, unpack)
    turned = lax.dot_general(
        eye_v[...], rows_v[...].astype(BF16), (((1,), (1,)), ((), ())), preferred_element_type=F32
    )
    half_lane = lax.broadcasted_iota(jnp.int32, (80, CH), 1) < 64
    packed_tail = jnp.where(half_lane, turned[0:80, 2 * CH :], turned[80:160, 2 * CH :])
    pieces_v[pid] = jnp.concatenate(
        [turned[:, :CH], turned[:, CH : 2 * CH], packed_tail], axis=0
    ).astype(BF16)

    def at(h, f, s):
        dx, dy = f * (1 - h) + s * h, f * h + s * (1 - h)
        return ((y + dy) % 4) * 4 + (x + dx) % 4

    def piece_copy(h, f, s, along, across, first, count, event):
        rows = pl.ds(pl.multiple_of(h * HR + first, 8), count)
        return pltpu.make_async_remote_copy(
            src_ref=pieces_v.at[at(h, f, s), rows],
            dst_ref=pieces_v.at[at(h, f, s), rows],
            send_sem=q_ssem.at[0],
            recv_sem=q_rsem.at[event],
            device_id=plane_device(at(h, along, across)),
            device_id_type=MESH,
        )

    def wait_half(h, f, s, event):
        piece_copy(h, f, s, 1, 0, 0, HR, event).wait_recv()

    def rows_of(t, late):
        return ((0, FR), (FR, HR - FR))[t if late == 0 else 1 - t]

    def send_across(h, f):
        for late in range(2):
            for t in range(2):
                event = h * 11 + 3 + 2 * f + t if late == 0 else 27 + f
                piece_copy(h, f, 0, 0, 1 + 2 * t, *rows_of(t, late), event).start()

    def forward(h, f, s, along, t, event):
        first, count = ((0, FR), (FR, HR - FR))[t]
        step = 1 + 2 * t
        piece_copy(
            h, f, s, step if along else 0, 0 if along else step, first, count, event
        ).start()

    def own_half(h):
        for late in range(2):
            for t in range(2):
                event = h * 11 + t if late == 0 else 23 + 2 * h + t
                first, count = rows_of(t, late)
                piece_copy(h, 0, 0, 1 + 2 * t, 0, first, count, event).start()

    def near_along(h):
        for t in range(2):
            piece_copy(h, 3 - 2 * t, 0, 1, 0, *rows_of(t, 0), h * 11 + t).wait_recv()
            forward(h, 3 - 2 * t, 0, True, t, h * 11 + 2)

    def near_spread(h):
        for t in range(2):
            piece_copy(h, 3 - 2 * t, 0, 1, 0, *rows_of(t, 1), 23 + 2 * h + t).wait_recv()
            send_across(h, 3 - 2 * t)

    def near_across(h, f):
        for t in range(2):
            piece_copy(h, f, 3 - 2 * t, 1, 0, *rows_of(t, 0), h * 11 + 3 + 2 * f + t).wait_recv()
            forward(h, f, 3 - 2 * t, False, t, 22)

    def late_across(f):
        arrived(pieces_v.at[pl.ds(0, 1)], q_rsem.at[27 + f])

    def far_along(h):
        wait_half(h, 2, 0, h * 11 + 2)
        send_across(h, 2)

    repeat(2, own_half)
    repeat(2, lambda h: send_across(h, 0))
    relay_own(2)
    repeat(2, near_along)
    repeat(2, lambda h: near_across(h, 0))
    repeat(2, near_spread)
    repeat(2, far_along)
    relay_own(3)

    scale = 1.0 / math.sqrt(8 * NW)

    def put(k, lhs, rhs):
        both = jnp.dot(lhs, rhs, preferred_element_type=F32) * scale
        out_ref[pl.ds(2 * k, SHARE, stride=2 * NB), :] = both[:, :CH]
        out_ref[pl.ds(2 * k + 1, SHARE, stride=2 * NB), :] = both[:, CH:]

    def main_bin(k):
        lhs = jnp.concatenate([pieces_v[k, 0:SHARE], pieces_v[k, SHARE : 2 * SHARE]], axis=1)
        re, im = [], []
        for g in range(8):
            rows = own_v[g, k, 0:32]
            re.append(rows)
            im.append(rows[16:32])
            im.append(-rows[0:16])
        rhs = jnp.concatenate([jnp.concatenate(re, axis=0), jnp.concatenate(im, axis=0)], axis=1)
        put(k, lhs, rhs)

    sign = jnp.where(lax.broadcasted_iota(jnp.int32, (8, CH), 0) < 4, 1.0, -1.0).astype(F32)

    def tail_bin(kk):
        columns = []
        for pair in range(2):
            even = pieces_v[pair * 8 + kk, 2 * SHARE : QR].astype(F32)
            odd = pieces_v[pair * 8 + 4 + kk, 2 * SHARE : QR].astype(F32)
            upper = jnp.where(half_lane, even, pltpu.roll(odd, 64, axis=1))
            lower = jnp.where(half_lane, pltpu.roll(even, 64, axis=1), odd)
            columns.append(jnp.concatenate([upper, lower], axis=0))
        lhs = jnp.concatenate(columns, axis=1).astype(BF16)
        re, im = [], []
        for wh in range(4):
            for g in range(8):
                rows = own_v[g, wh * 4 + kk, 32:40].astype(F32)
                re.append(rows)
                im.append(pltpu.roll(rows, 4, axis=0) * sign)
        rhs = jnp.concatenate([jnp.concatenate(re, axis=0), jnp.concatenate(im, axis=0)], axis=1)
        put(MAIN + kk, lhs, rhs.astype(BF16))

    repeat(2, lambda h: near_across(h, 1))
    arrived(own_v.at[pl.ds(0, 4)], hand_sem.at[1])
    late_across(0)
    main_bin(pid)
    main_bin(at(0, 1, 0))
    repeat(2, lambda h: near_across(h, 3))
    main_bin(at(0, 3, 0))
    main_bin(at(0, 0, 1))
    repeat(2, lambda h: near_across(h, 2))
    main_bin(at(0, 0, 3))
    late_across(1)
    late_across(3)
    for f in (1, 3):
        for s in (1, 3):
            main_bin(at(0, f, s))
    late_across(2)
    arrived(pieces_v.at[pl.ds(0, 4)], q_rsem.at[22])
    for f, s in ((2, 0), (2, 1), (2, 2), (2, 3), (0, 2), (1, 2), (3, 2)):
        main_bin(at(0, f, s))
    unrolled(NB - MAIN, tail_bin)

    @pl.when(tm < 7)
    def _():
        halo_to(tm + 1).wait_send()

    lax.fori_loop(0, 7 - tm, lambda n, carry: (total_sent(n).wait_send(), carry)[1], 0)
    departed(first_v.at[pl.ds(0, 15)], a_sem.at[0])
    departed(shares_v.at[pl.ds(0, 15)], b_sem.at[0])
    departed(own_v.at[pl.ds(0, 4)], hand_sem.at[0])
    departed(pieces_v.at[pl.ds(0, 15)], q_ssem.at[0])
    for condition, group, other, slot in sends:

        @pl.when(condition)
        def _():
            own_copy(group, other, slot, own_rsem.at[0]).wait_send()


def body(raw_strain, source_blocks, band_bins):
    hbm = pl.BlockSpec(memory_space=pltpu.HBM)
    vmem = pl.BlockSpec(memory_space=pltpu.VMEM)
    dma = pltpu.SemaphoreType.DMA
    rows = pl.pallas_call(
        kernel,
        out_shape=jax.ShapeDtypeStruct((SHARE * NB * 2, CH), F32),
        in_specs=[hbm] * 2,
        out_specs=vmem,
        scratch_shapes=[
            pltpu.SMEM((4,), jnp.int32),
            pltpu.VMEM((4, DR, 512), BF16),
            pltpu.VMEM((MB, KB), BF16),
            pltpu.VMEM((EB, EB), BF16),
            pltpu.VMEM((RAW_PAD, CH), BF16),
            pltpu.VMEM((EN_PAD, CH), F32),
            pltpu.VMEM((EN_PAD, CH), BF16),
            pltpu.VMEM((EN_PAD, CH), F32),
            pltpu.VMEM((EN_PAD, CH), BF16),
            pltpu.VMEM((MAIN * AR, CH), F32),
            pltpu.VMEM((8, CH), F32),
            pltpu.VMEM((8, 8, CH), F32),
            pltpu.VMEM((8, MAIN, AR, CH), BF16),
            pltpu.VMEM((16, AR, CH), BF16),
            pltpu.VMEM((8, SR, CH), BF16),
            pltpu.VMEM((16, SR, CH), BF16),
            pltpu.VMEM((384, 256), F32),
            pltpu.VMEM((16, QR, CH), BF16),
            pltpu.VMEM((EB, CH), F32),
            pltpu.VMEM((2, MB, CH), F32),
            pltpu.VMEM((SHARE, 256), BF16),
            dma((2,)),
            dma((6,)),
            dma((2,)),
            dma((7,)),
            dma((7,)),
            dma((2,)),
            dma((2,)),
            dma((6,)),
            dma((4,)),
            dma((2,)),
            dma((1,)),
            dma((31,)),
        ],
        compiler_params=pltpu.CompilerParams(
            collective_id=0, has_side_effects=True, vmem_limit_bytes=50 * 2**20
        ),
        name="cross_spectra",
    )(jnp.concatenate([source_blocks, band_bins]), raw_strain)
    return rows.reshape(SHARE, NB, 2, CH).transpose(0, 2, 1, 3).astype(BF16)


def solution(mesh):
    in_specs = (P("tm", "chan"), P(), P())
    out_specs = P("tm", None, None, "chan")
    return jax.shard_map(body, mesh=mesh, in_specs=in_specs, out_specs=out_specs, check_vma=False)
```

```python
import functools
import math

import jax
import jax.numpy as jnp
import numpy as np
from jax import lax
from jax.experimental import pallas as pl
from jax.experimental.pallas import tpu as pltpu
from jax.sharding import PartitionSpec as P

NW = 16
WIN = 500
NB = 20
VS = 640
TAPS = 64
DECIM = 4
CH = 128
ROWS = DECIM * NW * WIN
OUTS = NW * WIN
MB = 112
KB = 512
STEP = DECIM * MB
PAIRS = 36
HALO = 64
RAW_PAD = HALO + 2 * PAIRS * STEP
DEC_PAD = 2 * PAIRS * MB
EB = 256
EN_PAD = 8192
CHUNKS = (0, 6272, 11648, 17024, 22400, 27776, ROWS)
DR = 48
MAIN = 16
AR = 40
SR = 56
QR = 400
SHARE = 160
HR = QR // 2
FAR_FIRST = sorted(
    ((dy, dx) for dy in range(4) for dx in range(4) if dy or dx),
    key=lambda step: (-min(step[0], 4 - step[0]) - min(step[1], 4 - step[1]), step),
)
FR = 104
FORGET = math.exp(-1.0 / WIN)
F32 = jnp.float32
BF16 = jnp.bfloat16
MESH = pl.DeviceIdType.MESH


def lowpass_taps():
    offsets = np.arange(TAPS) - (TAPS - 1) / 2.0
    window = 0.54 - 0.46 * np.cos(2.0 * np.pi * np.arange(TAPS) / (TAPS - 1))
    angles = np.pi * 0.8 * offsets / DECIM
    values = np.sin(angles) / angles * window
    return values / values.sum()


def make_filter(filter_v):
    taps = lowpass_taps().astype(jnp.bfloat16).astype(np.float32)
    row = lax.broadcasted_iota(jnp.int32, (8, CH), 0)
    lane = lax.broadcasted_iota(jnp.int32, (8, CH), 1)
    lag = DECIM * row + DECIM - 1 + HALO - lane
    eight = jnp.zeros((8, CH), F32)
    for j in range(TAPS):
        eight = jnp.where(lag == j, float(taps[j]), eight)
    for b in range(MB // 16):
        rows = []
        for half in range(2):
            shift = 32 * (2 * b + half)
            turned = pltpu.roll(eight, shift % CH, axis=1) if shift % CH else eight
            columns = []
            for q in range(KB // CH):
                if q == shift // CH:
                    columns.append(jnp.where(lane >= shift % CH, turned, 0.0))
                elif q == shift // CH + 1:
                    columns.append(jnp.where(lane < shift % CH, turned, 0.0))
                else:
                    columns.append(jnp.zeros((8, CH), F32))
            rows.append(jnp.concatenate(columns, axis=1))
        filter_v[16 * b : 16 * b + 16, :] = jnp.concatenate(rows, axis=0).astype(BF16)


def make_tables(table_v, within_v, rising_v):
    place = lax.broadcasted_iota(jnp.int32, (EB, CH), 0).astype(F32)
    rising_v[...] = jnp.exp((place + 1.0) * (-1.0 / WIN))
    gap = lax.broadcasted_iota(jnp.int32, (EB, EB), 0) - lax.broadcasted_iota(jnp.int32, (EB, EB), 1)
    share = (1.0 - FORGET) * jnp.exp(jnp.maximum(gap, 0).astype(F32) * (-1.0 / WIN))
    within_v[...] = jnp.where(gap >= 0, share, 0.0).astype(BF16)
    row = lax.broadcasted_iota(jnp.int32, (DR, 512), 0)
    time = lax.broadcasted_iota(jnp.int32, (DR, 512), 1)
    late = row >= 2 * MAIN
    bin_id = jnp.where(late, MAIN + row % 4, row % MAIN)
    quarter = jnp.where(late, row // 4 % 2, row // MAIN % 2)
    angle = ((bin_id + 1) * time + (WIN // 4) * quarter).astype(F32)
    angle = angle - jnp.floor(angle * (1.0 / WIN)) * WIN
    angle = jnp.where(angle < 0.0, angle + WIN, jnp.where(angle >= WIN, angle - WIN, angle))
    angle = jnp.minimum(angle, WIN - angle)
    flip = angle > WIN / 4.0
    angle = jnp.where(flip, WIN / 2.0 - angle, angle)
    square = (angle * angle) * ((2.0 * math.pi / WIN) ** 2)
    cosine = jnp.full((DR, 512), 1.0, F32)
    for order in (14, 12, 10, 8, 6, 4, 2):
        cosine = 1.0 - square * cosine * (1.0 / (order * (order - 1)))
    cosine = jnp.where(flip, -cosine, cosine) * (1.0 / math.sqrt(WIN))
    cosine = jnp.where((time < WIN) & (row < 2 * NB), cosine, 0.0)
    for place in range(4):
        shifted = pltpu.roll(cosine, 4 * place, axis=1) if place else cosine
        table_v[place] = shifted.astype(BF16)


def kernel(
    small_hbm, raw_ref, out_ref,
    blocks_ref, table_v, filter_v, within_v, raw_v, dec_v, en_v, run_v, norm_v, white_v, total_v, totals_v,
    own_v, first_v, share_v, shares_v, rows_v, pieces_v, rising_v, weights_v, eye_v,
    small_sem, raw_sem, halo_sem, tot_ssem, tot_rsem, a_sem, b_sem, own_ssem, own_rsem, hand_sem, q_ssem, q_rsem,
):
    tm = lax.axis_index("tm")
    chan = lax.axis_index("chan")
    zl, core = tm // 2, tm % 2
    zh, pid = chan // 16, chan % 16
    y, x = pid // 4, pid % 4
    line = zh * 8 + tm
    totals_v[...] = jnp.zeros(totals_v.shape, F32)

    def repeat(count, step):
        lax.fori_loop(0, count, lambda n, carry: (step(n), carry)[1], 0)

    def unrolled(count, step):
        for n in range(count):
            step(n)

    def plane_device(other):
        return (tm, zh * 16 + other)

    def line_device(other):
        return (other % 8, (other // 8) * 16 + pid)

    def chunk(c):
        first, last = CHUNKS[c], CHUNKS[c + 1]
        return pltpu.make_async_copy(
            raw_ref.at[pl.ds(first, last - first)],
            raw_v.at[pl.ds(HALO + first, last - first)],
            raw_sem.at[c],
        )

    small = [
        pltpu.make_async_copy(source, target, small_sem.at[n])
        for n, (source, target) in enumerate(
            ((small_hbm, blocks_ref),)
        )
    ]
    for c in range(6):
        chunk(c).start()
    small[0].start()

    barrier = pltpu.get_barrier_semaphore()

    def greet(n):
        pl.semaphore_signal(
            barrier, inc=1, device_id=line_device((line + n + 1) % 16), device_id_type=MESH
        )
        pl.semaphore_signal(
            barrier, inc=1, device_id=plane_device((pid + n + 1) % 16), device_id_type=MESH
        )

    repeat(15, greet)

    raw_v[HALO + ROWS : RAW_PAD, :] = jnp.zeros((RAW_PAD - HALO - ROWS, CH), BF16)
    en_v[DEC_PAD:EN_PAD, :] = jnp.zeros((EN_PAD - DEC_PAD, CH), BF16)
    dec_v[DEC_PAD:EN_PAD, :] = jnp.zeros((EN_PAD - DEC_PAD, CH), F32)

    @pl.when(tm == 0)
    def _():
        raw_v[0:HALO, :] = jnp.zeros((HALO, CH), BF16)

    def halo_to(other):
        return pltpu.make_async_remote_copy(
            src_ref=raw_ref.at[pl.ds(ROWS - HALO, HALO)],
            dst_ref=raw_v.at[pl.ds(0, HALO)],
            send_sem=halo_sem.at[0],
            recv_sem=halo_sem.at[1],
            device_id=(other, chan),
            device_id_type=MESH,
        )

    tail = OUTS - (2 * PAIRS - 1) * MB
    back = lax.broadcasted_iota(jnp.int32, (MB, CH), 0).astype(F32) - (MB - 1.0)
    weights_v[0] = (1.0 - FORGET) * jnp.exp(back * (1.0 / WIN))
    back = back + float(MB - tail)
    weights_v[1] = jnp.where(
        back <= 0.0, (1.0 - FORGET) * jnp.exp(jnp.minimum(back, 0.0) * (1.0 / WIN)), 0.0
    )
    make_filter(filter_v)

    block_fade = FORGET**MB
    tail_fade = FORGET**tail

    def decimate(n, total):
        pair = (n + 1) % PAIRS
        is_tail, is_first = pair == PAIRS - 1, pair == 0
        start = pl.multiple_of(pair * (2 * STEP), 128)
        left = raw_v[pl.ds(start, KB), :]
        right = raw_v[pl.ds(start + STEP, KB), :]
        both = jnp.dot(
            filter_v[...], jnp.concatenate([left, right], axis=1), preferred_element_type=F32
        )
        row = pl.multiple_of(pair * (2 * MB), 32)
        sums = []
        for half in range(2):
            values = both[:, half * CH : (half + 1) * CH]
            dec_v[pl.ds(row + half * MB, MB), :] = values
            energy = values * values
            en_v[pl.ds(row + half * MB, MB), :] = energy.astype(BF16)
            weights = weights_v[0] if half == 0 else weights_v[pair // (PAIRS - 1)]
            sums.append(jnp.sum((weights * energy).reshape(MB // 8, 8, CH), axis=0))
        fade = jnp.where(is_tail, tail_fade, block_fade).astype(F32)
        decay = jnp.where(is_first, 1.0, block_fade * fade).astype(F32)
        gain = jnp.where(is_first, FORGET ** (OUTS - 2 * MB), 1.0).astype(F32)
        return total * decay + (sums[0] * fade + sums[1]) * gain

    def two_pairs(n, total):
        return decimate(n + 1, decimate(n, total))

    def stretch(c, total):
        for n in range(6):

            @pl.when(c == n)
            def _():
                chunk(n).wait()

        @pl.when(c == 4)
        def _():
            pl.semaphore_wait(barrier, 30)

            @pl.when(tm < 7)
            def _():
                halo_to(tm + 1).start()

        @pl.when((c == 5) & (tm > 0))
        def _():
            halo_to(tm - 1).wait_recv()

        return lax.fori_loop(0, 3, lambda n, t: two_pairs(6 * c + 2 * n, t), total)

    total = lax.fori_loop(0, 6, stretch, jnp.zeros((8, CH), F32))
    total_v[...] = jnp.broadcast_to(jnp.sum(total, axis=0, keepdims=True), (8, CH))

    def total_to(other, group, slot):
        return pltpu.make_async_remote_copy(
            src_ref=total_v,
            dst_ref=totals_v.at[group],
            send_sem=tot_ssem.at[slot],
            recv_sem=tot_rsem.at[group],
            device_id=(other, chan),
            device_id_type=MESH,
        )

    def total_sent(n):
        return total_to(tm + 1 + n, tm, n)

    lax.fori_loop(0, 7 - tm, lambda n, carry: (total_sent(n).start(), carry)[1], 0)
    make_tables(table_v, within_v, rising_v)

    def arrived(ref, sem):
        pltpu.make_async_remote_copy(
            src_ref=ref, dst_ref=ref, send_sem=sem, recv_sem=sem,
            device_id=plane_device((pid + 1) % 16), device_id_type=MESH,
        ).wait_recv()

    def departed(ref, sem):
        pltpu.make_async_remote_copy(
            src_ref=ref, dst_ref=ref, send_sem=sem, recv_sem=sem,
            device_id=plane_device((pid + 1) % 16), device_id_type=MESH,
        ).wait_send()

    def local_run(n):
        row = pl.multiple_of(n * (2 * EB), 2 * EB)
        rhs = jnp.concatenate([en_v[pl.ds(row, EB), :], en_v[pl.ds(row + EB, EB), :]], axis=1)
        both = jnp.dot(within_v[...], rhs, preferred_element_type=F32)
        run_v[pl.ds(row, EB), :] = both[:, :CH]
        run_v[pl.ds(row + EB, EB), :] = both[:, CH:]

    repeat(EN_PAD // (4 * EB), lambda n: (local_run(2 * n), local_run(2 * n + 1)))

    def total_taken(group, carry):
        total_to((tm + 1) % 8, group, 0).wait_recv()
        return carry

    lax.fori_loop(0, tm, total_taken, 0)

    state = jnp.zeros((8, CH), F32)
    for group in range(7):
        state = jnp.where(group < tm, state * math.exp(-NW) + totals_v[group], state)

    def normalize(block, state):
        row = pl.multiple_of(block * EB, EB)
        running = run_v[pl.ds(row, EB), :] + rising_v[...] * state[0:1, :]
        values = dec_v[pl.ds(row, EB), :] * lax.rsqrt(jnp.maximum(running, 0.01))
        norm_v[pl.ds(row, EB), :] = values.astype(BF16)
        return jnp.broadcast_to(running[EB - 1 : EB, :], (8, CH))

    lax.fori_loop(
        0, EN_PAD // (2 * EB), lambda n, s: normalize(2 * n + 1, normalize(2 * n, s)), state
    )

    small[0].wait()
    low, high = blocks_ref[2], blocks_ref[3]
    row_id = lax.broadcasted_iota(jnp.int32, (2 * NB, CH), 0)
    bin_id = jnp.where(row_id < 2 * MAIN, row_id % MAIN, MAIN + row_id % 4)
    keep = jnp.where((bin_id >= low) & (bin_id < high), 1.0, 0.0).astype(F32)

    def spectra_of(n):
        first = n + n // 4 * 4
        start = first * WIN // 16 * 16
        rhs = jnp.concatenate(
            [norm_v[pl.ds(start, 512), :], norm_v[pl.ds(start + 4 * WIN, 512), :]], axis=1
        )
        both = jnp.dot(table_v[first * WIN % 16 // 4], rhs, preferred_element_type=F32)
        for half in range(2):
            w = first + 4 * half
            spectra = both[: 2 * NB, half * CH : (half + 1) * CH]
            power = jnp.sum(spectra * spectra, axis=0, keepdims=True) / NB
            white = spectra * keep * lax.rsqrt(jnp.maximum(power, 0.1))
            for p in range(2):
                white_v[pl.ds(p * NW + w, MAIN, stride=AR), :] = white[p * MAIN : (p + 1) * MAIN]
                white_v[pl.ds(w // 4 * (4 * AR) + 32 + p * 4 + w % 4, 4, stride=AR), :] = white[
                    32 + 4 * p : 36 + 4 * p
                ]

    unrolled(8, spectra_of)
    own_v[tm] = white_v[...].reshape(MAIN, AR, CH).astype(BF16)

    def plane_copy(other):
        return pltpu.make_async_remote_copy(
            src_ref=own_v.at[tm, other],
            dst_ref=first_v.at[pid],
            send_sem=a_sem.at[0],
            recv_sem=a_sem.at[1],
            device_id=plane_device(other),
            device_id_type=MESH,
        )

    for dy, dx in FAR_FIRST:
        plane_copy((y + dy) % 4 * 4 + (x + dx) % 4).start()

    def own_copy(group, other, slot, arrival):
        return pltpu.make_async_remote_copy(
            src_ref=own_v.at[group],
            dst_ref=own_v.at[group],
            send_sem=own_ssem.at[slot],
            recv_sem=arrival,
            device_id=(other, chan),
            device_id_type=MESH,
        )

    partner = zl * 2 + 1 - core

    def hand_over(group):
        return pltpu.make_async_remote_copy(
            src_ref=own_v.at[group],
            dst_ref=own_v.at[group],
            send_sem=hand_sem.at[0],
            recv_sem=hand_sem.at[1],
            device_id=(partner, chan),
            device_id_type=MESH,
        )

    sends = []

    def send_along(condition, group, other, slot):
        sends.append((condition, group, other, slot))

        @pl.when(condition)
        def _():
            own_copy(group, other, slot, own_rsem.at[group // 2]).start()

    send_along(zl < 3, tm, tm + 2, 0)
    send_along(zl > 0, tm, tm - 2, 1)
    hand_over(tm).start()

    def relay_own(step):
        below, above = tm - 2 * step, tm + 2 * step

        @pl.when(zl - step >= 0)
        def _():
            own_copy(below, partner, 0, own_rsem.at[below // 2]).wait_recv()

        @pl.when(zl + step <= 3)
        def _():
            own_copy(above, partner, 0, own_rsem.at[above // 2]).wait_recv()

        if step < 3:
            send_along((zl - step >= 0) & (zl < 3), below, tm + 2, 2 * step)
            send_along((zl + step <= 3) & (zl > 0), above, tm - 2, 2 * step + 1)

        @pl.when(zl - step >= 0)
        def _():
            hand_over(below).start()

        @pl.when(zl + step <= 3)
        def _():
            hand_over(above).start()

    eye = (
        lax.broadcasted_iota(jnp.int32, (SHARE, 256), 0)
        == lax.broadcasted_iota(jnp.int32, (SHARE, 256), 1)
    )
    eye_v[...] = jnp.where(eye, 1.0, 0.0).astype(BF16)
    first_v[pid] = own_v[tm, pid]
    arrived(first_v.at[pl.ds(0, 15)], a_sem.at[1])

    lane8 = lax.broadcasted_iota(jnp.int32, (8, CH), 1)
    lane40 = lax.broadcasted_iota(jnp.int32, (AR, CH), 1)

    def turn_left(rows, lanes):
        return pltpu.roll(rows, CH - lanes, axis=1) if lanes else rows

    picked = []
    for b in range(2):
        for i in range(5):
            block = blocks_ref[b] + i
            here = jnp.where(block // 16 == zh, 1.0, 0.0).astype(F32)
            picked.append(first_v[block % 16].astype(F32) * here)
    for share in range(8):
        jj = share % 4
        a, c = picked[share // 4 * 5 + jj], picked[share // 4 * 5 + jj + 1]
        turned = turn_left(c, 32 * jj)
        head = jnp.where(lane40 < CH - 32 * jj, turn_left(a, 32 * jj), turned)
        rest = jnp.where(lane8 < 32, turned[0:8], 0.0)
        for q in range(1, 4):
            part = pltpu.roll(turned[8 * q : 8 * q + 8], 32 * q, axis=1)
            rest = jnp.where((lane8 >= 32 * q) & (lane8 < 32 * q + 32), part, rest)
        last_rest = jnp.where(lane8 < 32, turned[32:40], 0.0)
        share_v[share] = jnp.concatenate([head, rest, last_rest], axis=0).astype(BF16)

    def line_copy(other):
        return pltpu.make_async_remote_copy(
            src_ref=share_v.at[other % 8],
            dst_ref=shares_v.at[line],
            send_sem=b_sem.at[0],
            recv_sem=b_sem.at[1],
            device_id=line_device(other),
            device_id_type=MESH,
        )

    for dz in (4, 3, 5, 2, 6, 1, 7):
        for dc in range(2):
            line_copy((line // 2 + dz) % 8 * 2 + (core + dc) % 2).start()
    line_copy(line + 1 - 2 * core).start()
    shares_v[line] = share_v[tm]
    relay_own(1)
    arrived(shares_v.at[pl.ds(0, 15)], b_sem.at[1])

    def unpack(g):
        both = shares_v[g].astype(F32) + shares_v[8 + g].astype(F32)
        rests = [both[40:48]]
        for q in range(1, 4):
            rests.append(pltpu.roll(both[40:48], CH - 32 * q, axis=1))
        rests.append(both[48:56])
        rows = jnp.concatenate([both[0:40], jnp.concatenate(rests, axis=0)], axis=1)
        rows_v[pl.ds(pl.multiple_of(g * 32, 32), 32), :] = rows[0:32]
        rows_v[pl.ds(pl.multiple_of(256 + g * 8, 8), 8), :] = rows[32:40]
        rows_v[pl.ds(pl.multiple_of(320 + g * 8, 8), 8), :] = rows[32:40]

    unrolled(8, unpack)
    turned = lax.dot_general(
        eye_v[...], rows_v[...].astype(BF16), (((1,), (1,)), ((), ())), preferred_element_type=F32
    )
    half_lane = lax.broadcasted_iota(jnp.int32, (80, CH), 1) < 64
    packed_tail = jnp.where(half_lane, turned[0:80, 2 * CH :], turned[80:160, 2 * CH :])
    pieces_v[pid] = jnp.concatenate(
        [turned[:, :CH], turned[:, CH : 2 * CH], packed_tail], axis=0
    ).astype(BF16)

    def at(h, f, s):
        dx, dy = f * (1 - h) + s * h, f * h + s * (1 - h)
        return ((y + dy) % 4) * 4 + (x + dx) % 4

    def piece_copy(h, f, s, along, across, first, count, event):
        rows = pl.ds(pl.multiple_of(h * HR + first, 8), count)
        return pltpu.make_async_remote_copy(
            src_ref=pieces_v.at[at(h, f, s), rows],
            dst_ref=pieces_v.at[at(h, f, s), rows],
            send_sem=q_ssem.at[0],
            recv_sem=q_rsem.at[event],
            device_id=plane_device(at(h, along, across)),
            device_id_type=MESH,
        )

    def wait_half(h, f, s, event):
        piece_copy(h, f, s, 1, 0, 0, HR, event).wait_recv()

    def send_across(h, f):
        for t in range(2):
            piece_copy(h, f, 0, 0, 1 + 2 * t, 0, HR, h * 11 + 3 + 2 * f + t).start()

    def forward(h, f, s, along, t, event):
        first, count = ((0, FR), (FR, HR - FR))[t]
        step = 1 + 2 * t
        piece_copy(
            h, f, s, step if along else 0, 0 if along else step, first, count, event
        ).start()

    def along_rows(t, late):
        return ((0, FR), (FR, HR - FR))[t if late == 0 else 1 - t]

    def own_half(h):
        for late in range(2):
            for t in range(2):
                event = h * 11 + t if late == 0 else 23 + 2 * h + t
                first, count = along_rows(t, late)
                piece_copy(h, 0, 0, 1 + 2 * t, 0, first, count, event).start()

    def near_along(h):
        for t in range(2):
            piece_copy(h, 3 - 2 * t, 0, 1, 0, *along_rows(t, 0), h * 11 + t).wait_recv()
            forward(h, 3 - 2 * t, 0, True, t, h * 11 + 2)

    def near_spread(h):
        for t in range(2):
            piece_copy(h, 3 - 2 * t, 0, 1, 0, *along_rows(t, 1), 23 + 2 * h + t).wait_recv()
            send_across(h, 3 - 2 * t)

    def near_across(h, f):
        for t in range(2):
            wait_half(h, f, 3 - 2 * t, h * 11 + 3 + 2 * f + t)
            forward(h, f, 3 - 2 * t, False, t, 22)

    def far_along(h):
        wait_half(h, 2, 0, h * 11 + 2)
        send_across(h, 2)

    repeat(2, own_half)
    repeat(2, lambda h: send_across(h, 0))
    relay_own(2)
    repeat(2, near_along)
    repeat(2, lambda h: near_across(h, 0))
    repeat(2, near_spread)
    repeat(2, far_along)
    relay_own(3)

    scale = 1.0 / math.sqrt(8 * NW)

    def put(k, lhs, rhs):
        both = jnp.dot(lhs, rhs, preferred_element_type=F32) * scale
        out_ref[pl.ds(2 * k, SHARE, stride=2 * NB), :] = both[:, :CH]
        out_ref[pl.ds(2 * k + 1, SHARE, stride=2 * NB), :] = both[:, CH:]

    def main_bin(k):
        lhs = jnp.concatenate([pieces_v[k, 0:SHARE], pieces_v[k, SHARE : 2 * SHARE]], axis=1)
        re, im = [], []
        for g in range(8):
            rows = own_v[g, k, 0:32]
            re.append(rows)
            im.append(rows[16:32])
            im.append(-rows[0:16])
        rhs = jnp.concatenate([jnp.concatenate(re, axis=0), jnp.concatenate(im, axis=0)], axis=1)
        put(k, lhs, rhs)

    sign = jnp.where(lax.broadcasted_iota(jnp.int32, (8, CH), 0) < 4, 1.0, -1.0).astype(F32)

    def tail_bin(kk):
        columns = []
        for pair in range(2):
            even = pieces_v[pair * 8 + kk, 2 * SHARE : QR].astype(F32)
            odd = pieces_v[pair * 8 + 4 + kk, 2 * SHARE : QR].astype(F32)
            upper = jnp.where(half_lane, even, pltpu.roll(odd, 64, axis=1))
            lower = jnp.where(half_lane, pltpu.roll(even, 64, axis=1), odd)
            columns.append(jnp.concatenate([upper, lower], axis=0))
        lhs = jnp.concatenate(columns, axis=1).astype(BF16)
        re, im = [], []
        for wh in range(4):
            for g in range(8):
                rows = own_v[g, wh * 4 + kk, 32:40].astype(F32)
                re.append(rows)
                im.append(pltpu.roll(rows, 4, axis=0) * sign)
        rhs = jnp.concatenate([jnp.concatenate(re, axis=0), jnp.concatenate(im, axis=0)], axis=1)
        put(MAIN + kk, lhs, rhs.astype(BF16))

    repeat(2, lambda h: near_across(h, 1))
    arrived(own_v.at[pl.ds(0, 4)], hand_sem.at[1])
    main_bin(pid)
    main_bin(at(0, 1, 0))
    repeat(2, lambda h: near_across(h, 3))
    main_bin(at(0, 3, 0))
    main_bin(at(0, 0, 1))
    repeat(2, lambda h: near_across(h, 2))
    main_bin(at(0, 0, 3))
    for f in (1, 3):
        for s in (1, 3):
            main_bin(at(0, f, s))
    arrived(pieces_v.at[pl.ds(0, 4)], q_rsem.at[22])
    for f, s in ((2, 0), (2, 1), (2, 2), (2, 3), (0, 2), (1, 2), (3, 2)):
        main_bin(at(0, f, s))
    unrolled(NB - MAIN, tail_bin)

    @pl.when(tm < 7)
    def _():
        halo_to(tm + 1).wait_send()

    lax.fori_loop(0, 7 - tm, lambda n, carry: (total_sent(n).wait_send(), carry)[1], 0)
    departed(first_v.at[pl.ds(0, 15)], a_sem.at[0])
    departed(shares_v.at[pl.ds(0, 15)], b_sem.at[0])
    departed(own_v.at[pl.ds(0, 4)], hand_sem.at[0])
    departed(pieces_v.at[pl.ds(0, 15)], q_ssem.at[0])
    for condition, group, other, slot in sends:

        @pl.when(condition)
        def _():
            own_copy(group, other, slot, own_rsem.at[0]).wait_send()


def body(raw_strain, source_blocks, band_bins):
    hbm = pl.BlockSpec(memory_space=pltpu.HBM)
    vmem = pl.BlockSpec(memory_space=pltpu.VMEM)
    dma = pltpu.SemaphoreType.DMA
    rows = pl.pallas_call(
        kernel,
        out_shape=jax.ShapeDtypeStruct((SHARE * NB * 2, CH), F32),
        in_specs=[hbm] * 2,
        out_specs=vmem,
        scratch_shapes=[
            pltpu.SMEM((4,), jnp.int32),
            pltpu.VMEM((4, DR, 512), BF16),
            pltpu.VMEM((MB, KB), BF16),
            pltpu.VMEM((EB, EB), BF16),
            pltpu.VMEM((RAW_PAD, CH), BF16),
            pltpu.VMEM((EN_PAD, CH), F32),
            pltpu.VMEM((EN_PAD, CH), BF16),
            pltpu.VMEM((EN_PAD, CH), F32),
            pltpu.VMEM((EN_PAD, CH), BF16),
            pltpu.VMEM((MAIN * AR, CH), F32),
            pltpu.VMEM((8, CH), F32),
            pltpu.VMEM((8, 8, CH), F32),
            pltpu.VMEM((8, MAIN, AR, CH), BF16),
            pltpu.VMEM((16, AR, CH), BF16),
            pltpu.VMEM((8, SR, CH), BF16),
            pltpu.VMEM((16, SR, CH), BF16),
            pltpu.VMEM((384, 256), F32),
            pltpu.VMEM((16, QR, CH), BF16),
            pltpu.VMEM((EB, CH), F32),
            pltpu.VMEM((2, MB, CH), F32),
            pltpu.VMEM((SHARE, 256), BF16),
            dma((2,)),
            dma((6,)),
            dma((2,)),
            dma((7,)),
            dma((7,)),
            dma((2,)),
            dma((2,)),
            dma((6,)),
            dma((4,)),
            dma((2,)),
            dma((1,)),
            dma((27,)),
        ],
        compiler_params=pltpu.CompilerParams(
            collective_id=0, has_side_effects=True, vmem_limit_bytes=50 * 2**20
        ),
        name="cross_spectra",
    )(jnp.concatenate([source_blocks, band_bins]), raw_strain)
    return rows.reshape(SHARE, NB, 2, CH).transpose(0, 2, 1, 3).astype(BF16)


def solution(mesh):
    in_specs = (P("tm", "chan"), P(), P())
    out_specs = P("tm", None, None, "chan")
    return jax.shard_map(body, mesh=mesh, in_specs=in_specs, out_specs=out_specs, check_vma=False)
```
